512 devices in a mesh: tm: 64 (over y_hi, z, core), chan: 8 (over y_lo, x).
Axes of the slice: x: 4, y: 8 (y_hi: 4, y_lo: 2; y = y_hi * 2 + y_lo), z: 8, core: 2. Of those that a mesh axis runs over, the one named last changes fastest.
Arguments:
- samples: bfloat16 [32768, 4096], P('tm', 'chan'), may hold values from -6 to 6
- sketch: bfloat16 [4, 4096, 256], P(None, 'chan'), may hold values from -0.046875 to 0.046875
Outputs:
- image: float32 [8, 512, 4, 256], P('chan', 'tm')
The draws below stay inside these ranges and needn't reach their ends.
All inputs are finite; a program needn't handle non-finite values.
Results may differ from the reference program's by a relative error of at most 0.0029.
Values may be sent and summed in bfloat16 or wider, within the bound.
No kernel may reach another device: no remote copies, remote signals or barrier semaphores. Data moves between devices by JAX's collectives and lax.ppermute only.
A program may use at most 64 MiB of HBM per device.

```python
import jax
import jax.numpy as jnp

C = 4096
R = 256
P_SIZE = 4
SAMPLES = 32768
N_CHAN = 8


def block_scale(rng, shape, cuts, least, high):
    def one(dim, blocks):
        heights = jax.random.uniform(jax.random.fold_in(jax.random.fold_in(rng, 6), dim), (blocks,), jnp.float32, least / len(cuts), high / len(cuts))
        return jnp.repeat(jnp.exp(heights), shape[dim] // blocks).reshape((-1,) + (1,) * (len(shape) - dim - 1))

    level = one(*cuts[0])
    for cut in cuts[1:]:
        level = level * one(*cut)
    return level


def normal_values(stream_key, shape, width, bound, pieces=(), kind=jnp.bfloat16):
    result = jax.random.normal(stream_key, shape, jnp.float32) * width
    if len(pieces) > 0:
        result = block_scale(stream_key, shape, pieces, -0.22, 0.18) * result
    return jnp.clip(result, min=-bound, max=bound).astype(kind)


def setup_inputs(seed: int = 0) -> dict:
    key_list = jax.random.split(jax.random.key(seed), 3)
    return {
        "samples": normal_values(key_list[0], (SAMPLES, C), 1.0, 6.0, ((0, 64), (1, 8))),
        "sketch": normal_values(key_list[1], (P_SIZE, C, R), (P_SIZE * C) ** -0.5, 0.046875, ((1, 8),)),
    }


def reference(samples, sketch):
    count = samples.shape[0]
    span = 2 * P_SIZE - 1
    proj = jnp.einsum('tc,jcr->tjr', samples.astype(jnp.float32), sketch.astype(jnp.float32)).astype(jnp.bfloat16)
    padded = jnp.concatenate([samples, jnp.zeros((span, C), jnp.bfloat16)], 0)
    blocks = []
    for row_block in range(P_SIZE):
        total = jnp.zeros((C, R), jnp.float32)
        for column in range(P_SIZE):
            lag = P_SIZE + row_block - column
            window = padded[lag:lag + count]
            total = total + jnp.dot(window.T, proj[:, column], preferred_element_type=jnp.float32)
        blocks.append(total)
    stacked = jnp.stack(blocks, 1) / jnp.sqrt(jnp.float32(count))
    return stacked.reshape(N_CHAN, C // N_CHAN, P_SIZE, R)
```

```python
import functools

import jax
import jax.numpy as jnp
from jax import lax
from jax.experimental import pallas as pl
from jax.experimental.pallas import tpu as pltpu
from jax.sharding import Mesh
from jax.sharding import PartitionSpec as P

TM = ("y_hi", "z", "core")
CHAN = ("y_lo", "x")
EDGE = 8
LANES = 128


def in_vmem(kernel, out_shape, scratch=()):
    whole = pl.BlockSpec(memory_space=pltpu.VMEM)
    return lambda *args: pl.pallas_call(
        kernel,
        out_shape=out_shape,
        in_specs=[whole] * len(args),
        out_specs=whole,
        scratch_shapes=list(scratch),
        name=kernel.func.__name__ if isinstance(kernel, functools.partial) else kernel.__name__,
    )(*args)


def exchanged(pieces, axis):
    return lax.all_to_all(pieces, axis, split_axis=0, concat_axis=0, tiled=True)


def sketched(samples_ref, sketch_ref, out_ref, held):
    blocks = sketch_ref.shape[0]
    rows = samples_ref.shape[0]
    reach = out_ref.shape[0]
    for j in range(blocks):
        held[j, :EDGE] = jnp.zeros((EDGE, held.shape[2]), jnp.float32)
        held[j, EDGE + rows :] = jnp.zeros((held.shape[1] - EDGE - rows, held.shape[2]), jnp.float32)
        held[j, EDGE : EDGE + rows] = jnp.dot(
            samples_ref[...], sketch_ref[j], preferred_element_type=jnp.float32
        )
    total = held[blocks - 1, EDGE : EDGE + reach]
    for j in range(blocks - 1):
        start = EDGE - (blocks - 1 - j)
        total = total + held[j, start : start + reach]
    out_ref[...] = total


def copied(arrived_ref, out_ref):
    total = arrived_ref[0]
    for i in range(1, arrived_ref.shape[0]):
        total = total + arrived_ref[i]
    halves, copies, _, width = out_ref.shape
    for h in range(halves):
        for k in range(copies):
            out_ref[h, k] = total[:, h * width : (h + 1) * width]


def correlated(block_rows, rows, scale, turned_ref, sums_ref, out_ref, held):
    width = sums_ref.shape[2]
    reach = sums_ref.shape[1]
    depth = turned_ref.shape[1]
    held[...] = jnp.zeros_like(held)
    held[EDGE : EDGE + reach] = sums_ref[0]
    for k in range(1, sums_ref.shape[0]):
        start = EDGE + k * rows
        held[start : start + reach] = held[start : start + reach] + sums_ref[k]
    for i in range(block_rows):
        wide = held[EDGE - 1 - i : EDGE - 1 - i + depth]
        high = wide.astype(jnp.bfloat16)
        low = (wide - high.astype(jnp.float32)).astype(jnp.bfloat16)
        found = jnp.dot(turned_ref[...], high, preferred_element_type=jnp.float32)
        found = found + jnp.dot(turned_ref[...], low, preferred_element_type=jnp.float32)
        out_ref[:, i * width : (i + 1) * width] = (found * scale).astype(out_ref.dtype)


def shards(samples, sketch):
    rows, local = samples.shape
    blocks, _, width = sketch.shape
    cores = lax.axis_size("core")
    near = lax.axis_size(CHAN)
    groups = lax.axis_size(TM)
    half = width // cores
    part = -(-(rows + blocks - 1) // (near * EDGE)) * EDGE
    reach = near * part
    depth = cores * rows + 2 * EDGE

    other = lax.ppermute(samples, "core", [(i, cores - 1 - i) for i in range(cores)])
    first = lax.axis_index("core") == 0
    chip = jnp.where(
        first, jnp.concatenate([samples, other], 0), jnp.concatenate([other, samples], 0)
    )
    ahead = lax.ppermute(chip[:EDGE], TM, [(i + cores, i) for i in range(groups - cores)])
    tail = jnp.zeros((depth - cores * rows - EDGE, local), samples.dtype)
    turned = jnp.concatenate([chip, ahead, tail], 0).T

    partial = in_vmem(
        sketched,
        jax.ShapeDtypeStruct((reach, width), jnp.float32),
        [pltpu.VMEM((blocks, reach + 2 * EDGE, width), jnp.float32)],
    )(samples, sketch)
    arrived = exchanged(partial.reshape(near, part, width), CHAN)
    copies = in_vmem(copied, jax.ShapeDtypeStruct((cores, near, part, half), jnp.float32))(arrived)
    sums = exchanged(copies.reshape(cores * near, part, half), ("core", *CHAN))
    scale = 1.0 / (rows * groups) ** 0.5
    found = in_vmem(
        functools.partial(correlated, blocks, rows, scale),
        jax.ShapeDtypeStruct((local, blocks * half), jnp.bfloat16),
        [pltpu.VMEM((EDGE + (cores - 1) * rows + reach + 2 * EDGE, half), jnp.float32)],
    )(turned, sums.reshape(cores, reach, half))
    landed = exchanged(found.reshape(groups, local // groups, blocks * half), TM)
    landed = landed.reshape(groups // cores, cores, local // groups, blocks, half)
    mine = landed.astype(jnp.float32).sum(0)
    return jnp.moveaxis(mine, 0, 2).reshape(1, local // groups, blocks, width)


def solution(mesh):
    sizes = {"y_hi": 4, "z": 8, "core": 2, "y_lo": 2, "x": 4}
    fine = Mesh(mesh.devices.reshape(tuple(sizes.values())), tuple(sizes))
    placed = (P(TM, CHAN), P(None, CHAN, None))
    return jax.shard_map(
        shards, mesh=fine, in_specs=placed, out_specs=P(CHAN, TM, None, None), check_vma=False
    )
```

```python
import functools

import jax
import jax.numpy as jnp
from jax import lax
from jax.experimental import pallas as pl
from jax.experimental.pallas import tpu as pltpu
from jax.sharding import Mesh
from jax.sharding import PartitionSpec as P

TM = ("y_hi", "z", "core")
CHAN = ("y_lo", "x")
EDGE = 8
ROOT_SCALE = 512.0


def in_vmem(name, kernel, out_shape, scratch=()):
    whole = pl.BlockSpec(memory_space=pltpu.VMEM)
    return lambda *args: pl.pallas_call(
        kernel,
        out_shape=out_shape,
        in_specs=[whole] * len(args),
        out_specs=whole,
        scratch_shapes=list(scratch),
        name=name,
    )(*args)


def exchanged(pieces, axis):
    return lax.all_to_all(pieces, axis, split_axis=0, concat_axis=0, tiled=True)


def coded(values):
    root = jnp.sqrt(jnp.abs(values)) * ROOT_SCALE
    return jnp.where(values < 0, -root, root).astype(jnp.float16)


def decoded(codes):
    root = codes.astype(jnp.float32) * (1.0 / ROOT_SCALE)
    return root * jnp.abs(root)


def sketched(samples_ref, sketch_ref, out_ref, held):
    blocks = sketch_ref.shape[0]
    rows = samples_ref.shape[0]
    reach = out_ref.shape[0]
    for j in range(blocks):
        held[j, :EDGE] = jnp.zeros((EDGE, held.shape[2]), jnp.float32)
        held[j, EDGE + rows :] = jnp.zeros((held.shape[1] - EDGE - rows, held.shape[2]), jnp.float32)
        held[j, EDGE : EDGE + rows] = jnp.dot(
            samples_ref[...], sketch_ref[j], preferred_element_type=jnp.float32
        )
    total = held[blocks - 1, EDGE : EDGE + reach]
    for j in range(blocks - 1):
        start = EDGE - (blocks - 1 - j)
        total = total + held[j, start : start + reach]
    out_ref[...] = total


def correlated(block_rows, scale, own_ref, other_ref, tail_ref, sums_ref, out_ref, held, high, low):
    cores, reach, width = sums_ref.shape
    rows = own_ref.shape[1]
    depth = high.shape[0]
    held[...] = jnp.zeros_like(held)
    held[EDGE : EDGE + reach] = sums_ref[0]
    for k in range(1, cores):
        start = EDGE + k * rows
        held[start : start + reach] = held[start : start + reach] + sums_ref[k]
    for i in range(block_rows):
        wide = held[EDGE - 1 - i : EDGE - 1 - i + depth]
        part = wide.astype(jnp.bfloat16)
        high[:, i * width : (i + 1) * width] = part
        low[:, i * width : (i + 1) * width] = (wide - part.astype(jnp.float32)).astype(jnp.bfloat16)
    core = lax.axis_index("core")
    mine = pl.ds(pl.multiple_of(core * rows, rows), rows)
    theirs = pl.ds(pl.multiple_of((cores - 1 - core) * rows, rows), rows)
    ends = pl.ds(cores * rows, depth - cores * rows)
    found = jnp.zeros(out_ref.shape, jnp.float32)
    for turned, where in ((own_ref, mine), (other_ref, theirs), (tail_ref, ends)):
        for sums in (high, low):
            found = found + jnp.dot(turned[...], sums[where], preferred_element_type=jnp.float32)
    out_ref[...] = (found * scale).astype(out_ref.dtype)


def landed_sum(block_rows, landed_ref, out_ref):
    senders, cores, _, length = landed_ref.shape
    half = length // block_rows
    for k in range(cores):
        total = landed_ref[0, k].astype(jnp.float32)
        for n in range(1, senders):
            total = total + landed_ref[n, k].astype(jnp.float32)
        for i in range(block_rows):
            out_ref[0, :, i, k * half : (k + 1) * half] = total[:, i * half : (i + 1) * half]


def shards(samples, sketch):
    rows, local = samples.shape
    blocks, _, width = sketch.shape
    cores = lax.axis_size("core")
    near = lax.axis_size(CHAN)
    groups = lax.axis_size(TM)
    half = width // cores
    part = -(-(rows + blocks - 1) // (near * EDGE)) * EDGE
    reach = near * part
    depth = cores * rows + 2 * EDGE

    with jax.named_scope("head"):
        route = [(i + 1, i) for i in range(cores - 1, groups - 1, cores)]
        head = lax.ppermute(samples[:EDGE], TM, route)
    with jax.named_scope("sketched"):
        partial = in_vmem(
            "sketched",
            sketched,
            jax.ShapeDtypeStruct((reach, width), jnp.float32),
            [pltpu.VMEM((blocks, reach + 2 * EDGE, width), jnp.float32)],
        )(samples, sketch)
    partial, head = lax.optimization_barrier((partial, head))
    with jax.named_scope("swap"):
        swap = [(i, cores - 1 - i) for i in range(cores)]
        other = lax.ppermute(jnp.concatenate([samples, head], 0), "core", swap)
    with jax.named_scope("reduce"):
        arrived = exchanged(coded(partial).reshape(near, part, width), CHAN)
    arrived, other = lax.optimization_barrier((arrived, other))
    total = coded(decoded(arrived).sum(0))
    copies = [
        jnp.broadcast_to(total[None, :, k * half : (k + 1) * half], (near, part, half))
        for k in range(cores)
    ]
    with jax.named_scope("gather"):
        sums = exchanged(jnp.concatenate(copies, 0), ("core", *CHAN))
    first = lax.axis_index("core") == 0
    tail = jnp.where(first, other[rows:], head)
    tail = jnp.pad(tail, ((0, depth - cores * rows - EDGE), (0, 0)))
    scale = 1.0 / (rows * groups) ** 0.5
    found = in_vmem(
        "correlated",
        functools.partial(correlated, blocks, scale),
        jax.ShapeDtypeStruct((local, blocks * half), jnp.bfloat16),
        [
            pltpu.VMEM((EDGE + (cores - 1) * rows + reach + 2 * EDGE, half), jnp.float32),
            pltpu.VMEM((depth, blocks * half), jnp.bfloat16),
            pltpu.VMEM((depth, blocks * half), jnp.bfloat16),
        ],
    )(samples.T, other[:rows].T, tail.T, decoded(sums).reshape(cores, reach, half))
    with jax.named_scope("scatter"):
        landed = exchanged(found.reshape(groups, local // groups, blocks * half), TM)
    return in_vmem(
        "landed",
        functools.partial(landed_sum, blocks),
        jax.ShapeDtypeStruct((1, local // groups, blocks, width), jnp.float32),
    )(landed.reshape(groups // cores, cores, local // groups, blocks * half))


def solution(mesh):
    sizes = {"y_hi": 4, "z": 8, "core": 2, "y_lo": 2, "x": 4}
    fine = Mesh(mesh.devices.reshape(tuple(sizes.values())), tuple(sizes))
    placed = (P(TM, CHAN), P(None, CHAN, None))
    return jax.shard_map(
        shards, mesh=fine, in_specs=placed, out_specs=P(CHAN, TM, None, None), check_vma=False
    )
```

```python
import functools

import jax
import jax.numpy as jnp
from jax import lax
from jax.experimental import pallas as pl
from jax.experimental.layout import Layout, with_layout_constraint
from jax.experimental.pallas import tpu as pltpu
from jax.sharding import Mesh
from jax.sharding import PartitionSpec as P

TM = ("y_hi", "z", "core")
CHAN = ("y_lo", "x")
EDGE = 8
LANES = 128
ROOT_SCALE = 512.0
ANY = pl.BlockSpec(memory_space=pl.ANY)
VMEM = pl.BlockSpec(memory_space=pltpu.VMEM)


def local_kernel(name, kernel, out_shape, in_specs, scratch):
    return pl.pallas_call(
        kernel,
        out_shape=out_shape,
        in_specs=in_specs,
        out_specs=VMEM,
        scratch_shapes=scratch,
        name=name,
    )


def by_rows(array):
    return with_layout_constraint(array, Layout(tuple(range(array.ndim))))


def exchanged(pieces, axis):
    return lax.all_to_all(pieces, axis, split_axis=0, concat_axis=0, tiled=True)


def coded(values):
    root = jnp.sqrt(jnp.abs(values)) * ROOT_SCALE
    return jnp.where(values < 0, -root, root).astype(jnp.float16)


def decoded(codes):
    root = codes.astype(jnp.float32) * (1.0 / ROOT_SCALE)
    return root * jnp.abs(root)


def sketched(samples_hbm, sketch_hbm, out_ref, samples_ref, sketch_ref, held, arrivals):
    blocks = sketch_ref.shape[0]
    rows = samples_ref.shape[0]
    reach, width = out_ref.shape
    order = list(reversed(range(blocks)))
    loads = {j: pltpu.make_async_copy(sketch_hbm.at[j], sketch_ref.at[j], arrivals.at[j]) for j in order}
    first = pltpu.make_async_copy(samples_hbm, samples_ref, arrivals.at[blocks])
    first.start()
    for j in order:
        loads[j].start()
    for j in range(blocks):
        held[j, :EDGE] = jnp.zeros((EDGE, width), jnp.float32)
        held[j, EDGE + rows :] = jnp.zeros((held.shape[1] - EDGE - rows, width), jnp.float32)
    first.wait()
    for j in order:
        loads[j].wait()
        held[j, EDGE : EDGE + rows] = jnp.dot(
            samples_ref[...], sketch_ref[j], preferred_element_type=jnp.float32
        )
    total = held[blocks - 1, EDGE : EDGE + reach]
    for j in range(blocks - 1):
        start = EDGE - (blocks - 1 - j)
        total = total + held[j, start : start + reach]
    out_ref[...] = total


def correlated(
    block_rows, scale, own_hbm, other_hbm, tail_hbm, sums_ref, out_ref, turned, held, high, low, arrivals
):
    cores, reach, width = sums_ref.shape
    rows = own_hbm.shape[1]
    ends = tail_hbm.shape[1]
    core = lax.axis_index("core")
    mine = pl.ds(pl.multiple_of(core * rows, rows), rows)
    theirs = pl.ds(pl.multiple_of((cores - 1 - core) * rows, rows), rows)
    loads = [
        pltpu.make_async_copy(own_hbm, turned.at[:, mine], arrivals.at[0]),
        pltpu.make_async_copy(other_hbm, turned.at[:, theirs], arrivals.at[1]),
        pltpu.make_async_copy(tail_hbm, turned.at[:, cores * rows : cores * rows + ends], arrivals.at[2]),
    ]
    for load in loads:
        load.start()
    depth = cores * rows + 2 * EDGE
    held[:EDGE] = jnp.zeros((EDGE, width), jnp.float32)
    held[EDGE + reach :] = jnp.zeros((held.shape[0] - EDGE - reach, width), jnp.float32)
    held[EDGE : EDGE + reach] = sums_ref[0]
    for k in range(1, cores):
        start = EDGE + k * rows
        held[start : start + reach] = held[start : start + reach] + sums_ref[k]
    for sums in (high, low):
        sums[depth:] = jnp.zeros((sums.shape[0] - depth, sums.shape[1]), jnp.bfloat16)
    for i in range(block_rows):
        wide = held[EDGE - 1 - i : EDGE - 1 - i + depth]
        part = wide.astype(jnp.bfloat16)
        high[:depth, i * width : (i + 1) * width] = part
        low[:depth, i * width : (i + 1) * width] = (wide - part.astype(jnp.float32)).astype(jnp.bfloat16)
    for load in loads:
        load.wait()
    step = 2 * width
    for i in range(0, block_rows * width, step):
        found = jnp.dot(turned[...], high[:, i : i + step], preferred_element_type=jnp.float32)
        found = found + jnp.dot(turned[...], low[:, i : i + step], preferred_element_type=jnp.float32)
        out_ref[:, i : i + step] = (found * scale).astype(out_ref.dtype)


def shards(samples, sketch):
    rows, local = samples.shape
    blocks, _, width = sketch.shape
    cores = lax.axis_size("core")
    near = lax.axis_size(CHAN)
    groups = lax.axis_size(TM)
    half = width // cores
    part = -(-(rows + blocks - 1) // (near * EDGE)) * EDGE
    reach = near * part
    swap = [(i, cores - 1 - i) for i in range(cores)]
    ahead_route = [(i + cores, i) for i in range(groups - cores)]

    with jax.named_scope("swap"):
        other = by_rows(lax.ppermute(samples, "core", swap))
    partial = local_kernel(
        "sketched",
        sketched,
        jax.ShapeDtypeStruct((reach, width), jnp.float32),
        [ANY, ANY],
        [
            pltpu.VMEM(samples.shape, samples.dtype),
            pltpu.VMEM(sketch.shape, sketch.dtype),
            pltpu.VMEM((blocks, reach + 2 * EDGE, width), jnp.float32),
            pltpu.SemaphoreType.DMA((blocks + 1,)),
        ],
    )(samples, sketch)
    partial, other = lax.optimization_barrier((partial, other))
    with jax.named_scope("ahead"):
        first = lax.axis_index("core") == 0
        ahead = lax.ppermute(jnp.where(first, samples[:EDGE], other[:EDGE]), TM, ahead_route)
    with jax.named_scope("reduce"):
        arrived = exchanged(coded(partial).reshape(near, part, width), CHAN)
    arrived, ahead = lax.optimization_barrier((arrived, ahead))
    total = coded(decoded(arrived).sum(0))
    copies = [
        jnp.broadcast_to(total[None, :, k * half : (k + 1) * half], (near, part, half))
        for k in range(cores)
    ]
    with jax.named_scope("gather"):
        sums = exchanged(jnp.concatenate(copies, 0), ("core", *CHAN))
    tail = jnp.pad(ahead, ((0, LANES - EDGE), (0, 0)))
    scale = 1.0 / (rows * groups) ** 0.5
    found = local_kernel(
        "correlated",
        functools.partial(correlated, blocks, scale),
        jax.ShapeDtypeStruct((local, blocks * half), jnp.bfloat16),
        [ANY, ANY, ANY, VMEM],
        [
            pltpu.VMEM((local, cores * rows + LANES), samples.dtype),
            pltpu.VMEM((EDGE + (cores - 1) * rows + reach + 2 * EDGE, half), jnp.float32),
            pltpu.VMEM((cores * rows + LANES, blocks * half), jnp.bfloat16),
            pltpu.VMEM((cores * rows + LANES, blocks * half), jnp.bfloat16),
            pltpu.SemaphoreType.DMA((3,)),
        ],
    )(samples.T, other.T, tail.T, decoded(sums).reshape(cores, reach, half))
    with jax.named_scope("scatter"):
        landed = exchanged(found.reshape(groups, local // groups, blocks * half), TM)
    landed = landed.reshape(groups // cores, cores, local // groups, blocks, half)
    mine = landed.astype(jnp.float32).sum(0)
    return jnp.concatenate([mine[k] for k in range(cores)], -1)[None]


def solution(mesh):
    sizes = {"y_hi": 4, "z": 8, "core": 2, "y_lo": 2, "x": 4}
    fine = Mesh(mesh.devices.reshape(tuple(sizes.values())), tuple(sizes))
    placed = (P(TM, CHAN), P(None, CHAN, None))
    return jax.shard_map(
        shards, mesh=fine, in_specs=placed, out_specs=P(CHAN, TM, None, None), check_vma=False
    )
```

```python
import functools

import jax
import jax.numpy as jnp
from jax import lax
from jax.experimental import pallas as pl
from jax.experimental.layout import Layout, with_layout_constraint
from jax.experimental.pallas import tpu as pltpu
from jax.sharding import Mesh
from jax.sharding import PartitionSpec as P

TM = ("y_hi", "z", "core")
CHAN = ("y_lo", "x")
EDGE = 8
LANES = 128
ROOT_SCALE = 512.0
VMEM = pl.BlockSpec(memory_space=pltpu.VMEM)


def local_kernel(name, kernel, shape, dtype, scratch):
    def call(*args):
        args = [pltpu.with_memory_space_constraint(a, pltpu.VMEM) for a in args]
        return pl.pallas_call(
            kernel,
            out_shape=pltpu.VMEM(shape, dtype),
            in_specs=[VMEM] * len(args),
            out_specs=VMEM,
            scratch_shapes=scratch,
            name=name,
        )(*args)

    return call


def by_rows(array):
    return with_layout_constraint(array, Layout(tuple(range(array.ndim))))


def exchanged(pieces, axis):
    return lax.all_to_all(pieces, axis, split_axis=0, concat_axis=0, tiled=True)


def coded(values):
    root = jnp.sqrt(jnp.abs(values)) * ROOT_SCALE
    return jnp.where(values < 0, -root, root).astype(jnp.float16)


def decoded(codes):
    root = codes.astype(jnp.float32) * (1.0 / ROOT_SCALE)
    return root * jnp.abs(root)


def sketched(samples_ref, sketch_ref, out_ref, held):
    blocks = sketch_ref.shape[0]
    rows = samples_ref.shape[0]
    reach, width = out_ref.shape
    for j in range(blocks):
        held[j, :EDGE] = jnp.zeros((EDGE, width), jnp.float32)
        held[j, EDGE + rows :] = jnp.zeros((held.shape[1] - EDGE - rows, width), jnp.float32)
        held[j, EDGE : EDGE + rows] = jnp.dot(
            samples_ref[...], sketch_ref[j], preferred_element_type=jnp.float32
        )
    total = held[blocks - 1, EDGE : EDGE + reach]
    for j in range(blocks - 1):
        start = EDGE - (blocks - 1 - j)
        total = total + held[j, start : start + reach]
    out_ref[...] = total


def correlated(block_rows, scale, own_ref, other_ref, tail_ref, sums_ref, out_ref, held, high, low):
    cores, reach, width = sums_ref.shape
    rows = own_ref.shape[1]
    core = lax.axis_index("core")
    mine = pl.ds(pl.multiple_of(core * rows, rows), rows)
    theirs = pl.ds(pl.multiple_of((cores - 1 - core) * rows, rows), rows)
    ends = pl.ds(cores * rows, tail_ref.shape[1])
    depth = cores * rows + 2 * EDGE
    held[:EDGE] = jnp.zeros((EDGE, width), jnp.float32)
    held[EDGE + reach :] = jnp.zeros((held.shape[0] - EDGE - reach, width), jnp.float32)
    held[EDGE : EDGE + reach] = sums_ref[0]
    for k in range(1, cores):
        start = EDGE + k * rows
        held[start : start + reach] = held[start : start + reach] + sums_ref[k]
    for sums in (high, low):
        sums[depth:] = jnp.zeros((sums.shape[0] - depth, sums.shape[1]), jnp.bfloat16)
    for i in range(block_rows):
        wide = held[EDGE - 1 - i : EDGE - 1 - i + depth]
        part = wide.astype(jnp.bfloat16)
        high[:depth, i * width : (i + 1) * width] = part
        low[:depth, i * width : (i + 1) * width] = (wide - part.astype(jnp.float32)).astype(jnp.bfloat16)
    step = 2 * width
    for i in range(0, block_rows * width, step):
        found = jnp.zeros((out_ref.shape[0], step), jnp.float32)
        for turned, where in ((own_ref, mine), (other_ref, theirs), (tail_ref, ends)):
            for sums in (high, low):
                found = found + jnp.dot(
                    turned[...], sums[where, i : i + step], preferred_element_type=jnp.float32
                )
        out_ref[:, i : i + step] = (found * scale).astype(out_ref.dtype)


def shards(samples, sketch):
    rows, local = samples.shape
    blocks, _, width = sketch.shape
    cores = lax.axis_size("core")
    near = lax.axis_size(CHAN)
    groups = lax.axis_size(TM)
    half = width // cores
    part = -(-(rows + blocks - 1) // (near * EDGE)) * EDGE
    reach = near * part
    swap = [(i, cores - 1 - i) for i in range(cores)]
    ahead_route = [(i + cores, i) for i in range(groups - cores)]

    with jax.named_scope("swap"):
        other = by_rows(lax.ppermute(samples, "core", swap))
    partial = local_kernel(
        "sketched",
        sketched,
        (reach, width),
        jnp.float32,
        [pltpu.VMEM((blocks, reach + 2 * EDGE, width), jnp.float32)],
    )(samples, sketch)
    partial, other = lax.optimization_barrier((partial, other))
    with jax.named_scope("ahead"):
        first = lax.axis_index("core") == 0
        ahead = lax.ppermute(jnp.where(first, samples[:EDGE], other[:EDGE]), TM, ahead_route)
    with jax.named_scope("reduce"):
        arrived = exchanged(coded(partial).reshape(near, part, width), CHAN)
    arrived, ahead = lax.optimization_barrier((arrived, ahead))
    total = coded(decoded(arrived).sum(0))
    copies = [
        jnp.broadcast_to(total[None, :, k * half : (k + 1) * half], (near, part, half))
        for k in range(cores)
    ]
    with jax.named_scope("gather"):
        sums = exchanged(jnp.concatenate(copies, 0), ("core", *CHAN))
    tail = jnp.pad(ahead, ((0, LANES - EDGE), (0, 0)))
    scale = 1.0 / (rows * groups) ** 0.5
    found = local_kernel(
        "correlated",
        functools.partial(correlated, blocks, scale),
        (local, blocks * half),
        jnp.bfloat16,
        [
            pltpu.VMEM((EDGE + (cores - 1) * rows + reach + 2 * EDGE, half), jnp.float32),
            pltpu.VMEM((cores * rows + LANES, blocks * half), jnp.bfloat16),
            pltpu.VMEM((cores * rows + LANES, blocks * half), jnp.bfloat16),
        ],
    )(samples.T, other.T, tail.T, decoded(sums).reshape(cores, reach, half))
    with jax.named_scope("scatter"):
        landed = exchanged(found.reshape(groups, local // groups, blocks * half), TM)
    landed = landed.reshape(groups // cores, cores, local // groups, blocks, half)
    mine = landed.astype(jnp.float32).sum(0)
    return jnp.concatenate([mine[k] for k in range(cores)], -1)[None]


def solution(mesh):
    sizes = {"y_hi": 4, "z": 8, "core": 2, "y_lo": 2, "x": 4}
    fine = Mesh(mesh.devices.reshape(tuple(sizes.values())), tuple(sizes))
    placed = (P(TM, CHAN), P(None, CHAN, None))
    return jax.shard_map(
        shards, mesh=fine, in_specs=placed, out_specs=P(CHAN, TM, None, None), check_vma=False
    )
```

```python
import functools

import jax
import jax.numpy as jnp
from jax import lax
from jax.experimental import pallas as pl
from jax.experimental.layout import Layout, with_layout_constraint
from jax.experimental.pallas import tpu as pltpu
from jax.sharding import Mesh
from jax.sharding import PartitionSpec as P


TM = ("y_hi", "z", "core")
CHAN = ("y_lo", "x")
EDGE = 8
LANES = 128
ROOT_SCALE = 512.0
ANY = pl.BlockSpec(memory_space=pl.ANY)
VMEM = pl.BlockSpec(memory_space=pltpu.VMEM)


def local_kernel(kernel, shape, dtype, scratch, in_vmem=True):
    def call(*args):
        if in_vmem:
            args = [pltpu.with_memory_space_constraint(a, pltpu.VMEM) for a in args]
        return pl.pallas_call(
            kernel,
            out_shape=pltpu.VMEM(shape, dtype),
            in_specs=[VMEM if in_vmem else ANY] * len(args),
            out_specs=VMEM,
            scratch_shapes=scratch,
        )(*args)

    return call


def by_rows(array):
    return with_layout_constraint(array, Layout(tuple(range(array.ndim))))


def exchanged(pieces, axis):
    return lax.all_to_all(pieces, axis, split_axis=0, concat_axis=0, tiled=True)


def coded(values):
    root = jnp.sqrt(jnp.abs(values)) * ROOT_SCALE
    return jnp.where(values < 0, -root, root).astype(jnp.float16)


def decoded(codes):
    root = codes.astype(jnp.float32) * (1.0 / ROOT_SCALE)
    return root * jnp.abs(root)


def sketched(samples_hbm, sketch_hbm, out_ref, samples_ref, sketch_ref, held, arrivals):
    blocks = sketch_ref.shape[0]
    rows = samples_ref.shape[0]
    reach, width = out_ref.shape
    own = pltpu.make_async_copy(samples_hbm, samples_ref, arrivals.at[blocks])
    loads = [
        pltpu.make_async_copy(sketch_hbm.at[j], sketch_ref.at[j], arrivals.at[j])
        for j in range(blocks)
    ]
    own.start()
    for load in loads:
        load.start()
    for j in range(blocks):
        held[j, :EDGE] = jnp.zeros((EDGE, width), jnp.float32)
        held[j, EDGE + rows :] = jnp.zeros((held.shape[1] - EDGE - rows, width), jnp.float32)
    own.wait()
    for j in range(blocks):
        loads[j].wait()
        held[j, EDGE : EDGE + rows] = jnp.dot(
            samples_ref[...], sketch_ref[j], preferred_element_type=jnp.float32
        )
    total = held[blocks - 1, EDGE : EDGE + reach]
    for j in range(blocks - 1):
        start = EDGE - (blocks - 1 - j)
        total = total + held[j, start : start + reach]
    out_ref[...] = total


def correlated(block_rows, scale, own_ref, other_ref, tail_ref, sums_ref, out_ref, held, high, low):
    cores, reach, width = sums_ref.shape
    rows = own_ref.shape[1]
    core = lax.axis_index("core")
    mine = pl.ds(pl.multiple_of(core * rows, rows), rows)
    theirs = pl.ds(pl.multiple_of((cores - 1 - core) * rows, rows), rows)
    ends = pl.ds(cores * rows, tail_ref.shape[1])
    depth = cores * rows + 2 * EDGE
    held[:EDGE] = jnp.zeros((EDGE, width), jnp.float32)
    held[EDGE + reach :] = jnp.zeros((held.shape[0] - EDGE - reach, width), jnp.float32)
    held[EDGE : EDGE + reach] = sums_ref[0]
    for k in range(1, cores):
        start = EDGE + k * rows
        held[start : start + reach] = held[start : start + reach] + sums_ref[k]
    for sums in (high, low):
        sums[depth:] = jnp.zeros((sums.shape[0] - depth, sums.shape[1]), jnp.bfloat16)
    for i in range(block_rows):
        wide = held[EDGE - 1 - i : EDGE - 1 - i + depth]
        part = wide.astype(jnp.bfloat16)
        high[:depth, i * width : (i + 1) * width] = part
        low[:depth, i * width : (i + 1) * width] = (wide - part.astype(jnp.float32)).astype(jnp.bfloat16)
    step = 2 * width
    for i in range(0, block_rows * width, step):
        found = jnp.zeros((out_ref.shape[0], step), jnp.float32)
        for turned, where in ((own_ref, mine), (other_ref, theirs), (tail_ref, ends)):
            for sums in (high, low):
                found = found + jnp.dot(
                    turned[...], sums[where, i : i + step], preferred_element_type=jnp.float32
                )
        out_ref[:, i : i + step] = (found * scale).astype(out_ref.dtype)


def shards(samples, sketch):
    rows, local = samples.shape
    blocks, _, width = sketch.shape
    cores = lax.axis_size("core")
    near = lax.axis_size(CHAN)
    groups = lax.axis_size(TM)
    half = width // cores
    part = -(-(rows + blocks - 1) // (near * EDGE)) * EDGE
    reach = near * part
    swap = [(i, cores - 1 - i) for i in range(cores)]
    ahead_route = [(i + cores, i) for i in range(groups - cores)]

    other = by_rows(lax.ppermute(samples, "core", swap))
    partial = local_kernel(
        sketched,
        (reach, width),
        jnp.float32,
        [
            pltpu.VMEM(samples.shape, samples.dtype),
            pltpu.VMEM(sketch.shape, sketch.dtype),
            pltpu.VMEM((blocks, reach + 2 * EDGE, width), jnp.float32),
            pltpu.SemaphoreType.DMA((blocks + 1,)),
        ],
        in_vmem=False,
    )(samples, sketch)
    first = lax.axis_index("core") == 0
    ahead = lax.ppermute(jnp.where(first, samples[:EDGE], other[:EDGE]), TM, ahead_route)
    arrived = exchanged(coded(partial).reshape(near, part, width), CHAN)
    total = coded(decoded(arrived).sum(0))
    copies = [
        jnp.broadcast_to(total[None, :, k * half : (k + 1) * half], (near, part, half))
        for k in range(cores)
    ]
    sums = exchanged(jnp.concatenate(copies, 0), ("core", *CHAN))
    tail = jnp.pad(ahead, ((0, LANES - EDGE), (0, 0)))
    scale = 1.0 / (rows * groups) ** 0.5
    found = local_kernel(
        functools.partial(correlated, blocks, scale),
        (local, blocks * half),
        jnp.bfloat16,
        [
            pltpu.VMEM((EDGE + (cores - 1) * rows + reach + 2 * EDGE, half), jnp.float32),
            pltpu.VMEM((cores * rows + LANES, blocks * half), jnp.bfloat16),
            pltpu.VMEM((cores * rows + LANES, blocks * half), jnp.bfloat16),
        ],
    )(samples.T, other.T, tail.T, decoded(sums).reshape(cores, reach, half))
    landed = exchanged(found.reshape(groups, local // groups, blocks * half), TM)
    landed = landed.reshape(groups // cores, cores, local // groups, blocks, half)
    mine = landed.astype(jnp.float32).sum(0)
    return jnp.concatenate([mine[k] for k in range(cores)], -1)[None]


def solution(mesh):
    sizes = {"y_hi": 4, "z": 8, "core": 2, "y_lo": 2, "x": 4}
    fine = Mesh(mesh.devices.reshape(tuple(sizes.values())), tuple(sizes))
    placed = (P(TM, CHAN), P(None, CHAN, None))
    return jax.shard_map(
        shards, mesh=fine, in_specs=placed, out_specs=P(CHAN, TM, None, None), check_vma=False
    )
```

```python
import functools

import jax
import jax.numpy as jnp
from jax import lax
from jax.experimental import pallas as pl
from jax.experimental.layout import Layout, with_layout_constraint
from jax.experimental.pallas import tpu as pltpu
from jax.sharding import Mesh
from jax.sharding import PartitionSpec as P


TM = ("y_hi", "z", "core")
CHAN = ("y_lo", "x")
EDGE = 8
LANES = 128
ROOT_SCALE = 512.0
ANY = pl.BlockSpec(memory_space=pl.ANY)
VMEM = pl.BlockSpec(memory_space=pltpu.VMEM)


def local_kernel(kernel, out_shapes, scratch, in_vmem=True):
    def call(*args):
        if in_vmem:
            args = [pltpu.with_memory_space_constraint(a, pltpu.VMEM) for a in args]
        return pl.pallas_call(
            kernel,
            out_shape=[pltpu.VMEM(shape, dtype) for shape, dtype in out_shapes],
            in_specs=[VMEM if in_vmem else ANY] * len(args),
            out_specs=[VMEM] * len(out_shapes),
            scratch_shapes=scratch,
        )(*args)

    return call


def by_rows(array):
    return with_layout_constraint(array, Layout(tuple(range(array.ndim))))


def exchanged(pieces, axis):
    return lax.all_to_all(pieces, axis, split_axis=0, concat_axis=0, tiled=True)


def coded(values):
    root = jnp.sqrt(jnp.abs(values)) * ROOT_SCALE
    return jnp.where(values < 0, -root, root).astype(jnp.float16)


def decoded(codes):
    root = codes.astype(jnp.float32) * (1.0 / ROOT_SCALE)
    return root * jnp.abs(root)


def shifted_sum(held, reach, width):
    blocks = held.shape[1] // width
    total = held[EDGE : EDGE + reach, (blocks - 1) * width :]
    for j in range(blocks - 1):
        start = EDGE - (blocks - 1 - j)
        total = total + held[start : start + reach, j * width : (j + 1) * width]
    return total


def clear_edges(held, rows):
    held[:EDGE] = jnp.zeros((EDGE, held.shape[1]), jnp.float32)
    held[EDGE + rows :] = jnp.zeros((held.shape[0] - EDGE - rows, held.shape[1]), jnp.float32)


def sketched_own(samples_hbm, sketch_hbm, own_ref, columns_ref, samples_ref, held, arrivals):
    blocks = sketch_hbm.shape[0]
    rows = samples_ref.shape[0]
    reach, width = own_ref.shape
    start = pl.multiple_of(lax.axis_index("core") * width, width)
    rows_load = pltpu.make_async_copy(samples_hbm, samples_ref, arrivals.at[blocks])
    loads = [
        pltpu.make_async_copy(
            sketch_hbm.at[j, :, pl.ds(start, width)],
            columns_ref.at[:, j * width : (j + 1) * width],
            arrivals.at[j],
        )
        for j in range(blocks)
    ]
    rows_load.start()
    for load in loads:
        load.start()
    clear_edges(held, rows)
    rows_load.wait()
    for j in range(0, blocks, 2):
        pair = slice(j * width, (j + 2) * width)
        for load in loads[j : j + 2]:
            load.wait()
        held[EDGE : EDGE + rows, pair] = jnp.dot(
            samples_ref[...], columns_ref[:, pair], preferred_element_type=jnp.float32
        )
    own_ref[...] = shifted_sum(held, reach, width)


def sketched_chip(other_ref, columns_ref, own_ref, out_ref, held):
    rows = other_ref.shape[0]
    reach, width = own_ref.shape
    cores = (out_ref.shape[0] - EDGE) // rows
    clear_edges(held, rows)
    held[EDGE : EDGE + rows] = jnp.dot(
        other_ref[...], columns_ref[...], preferred_element_type=jnp.float32
    )
    core = lax.axis_index("core")
    mine = pl.ds(pl.multiple_of(core * rows, rows), reach)
    theirs = pl.ds(pl.multiple_of((cores - 1 - core) * rows, rows), reach)
    out_ref[...] = jnp.zeros_like(out_ref)
    out_ref[mine] = own_ref[...]
    out_ref[theirs] = out_ref[theirs] + shifted_sum(held, reach, width)


def correlated(block_rows, scale, own_ref, other_ref, tail_ref, sums_ref, out_ref, held, high, low):
    reach, width = sums_ref.shape
    rows = own_ref.shape[1]
    cores = reach // rows
    core = lax.axis_index("core")
    mine = pl.ds(pl.multiple_of(core * rows, rows), rows)
    theirs = pl.ds(pl.multiple_of((cores - 1 - core) * rows, rows), rows)
    ends = pl.ds(cores * rows, tail_ref.shape[1])
    depth = cores * rows + 2 * EDGE
    held[:EDGE] = jnp.zeros((EDGE, width), jnp.float32)
    held[EDGE:] = sums_ref[...]
    for sums in (high, low):
        sums[depth:] = jnp.zeros((sums.shape[0] - depth, sums.shape[1]), jnp.bfloat16)
    for i in range(block_rows):
        wide = held[EDGE - 1 - i : EDGE - 1 - i + depth]
        part = wide.astype(jnp.bfloat16)
        high[:depth, i * width : (i + 1) * width] = part
        low[:depth, i * width : (i + 1) * width] = (wide - part.astype(jnp.float32)).astype(jnp.bfloat16)
    step = 2 * width
    for i in range(0, block_rows * width, step):
        found = jnp.zeros((out_ref.shape[0], step), jnp.float32)
        for turned, where in ((own_ref, mine), (other_ref, theirs), (tail_ref, ends)):
            for sums in (high, low):
                found = found + jnp.dot(
                    turned[...], sums[where, i : i + step], preferred_element_type=jnp.float32
                )
        out_ref[:, i : i + step] = (found * scale).astype(out_ref.dtype)


def shards(samples, sketch):
    rows, local = samples.shape
    blocks, _, width = sketch.shape
    cores = lax.axis_size("core")
    near = lax.axis_size(CHAN)
    groups = lax.axis_size(TM)
    half = width // cores
    part = -(-(cores * rows + blocks - 1) // (near * EDGE)) * EDGE
    reach = near * part
    swap = [(i, cores - 1 - i) for i in range(cores)]
    ahead_route = [(i + cores, i) for i in range(groups - cores)]

    other = by_rows(lax.ppermute(samples, "core", swap))
    held = pltpu.VMEM((rows + 3 * EDGE, blocks * half), jnp.float32)
    own, columns = local_kernel(
        sketched_own,
        [((rows + EDGE, half), jnp.float32), ((local, blocks * half), sketch.dtype)],
        [pltpu.VMEM(samples.shape, samples.dtype), held, pltpu.SemaphoreType.DMA((blocks + 1,))],
        in_vmem=False,
    )(samples, sketch)
    (partial,) = local_kernel(
        sketched_chip, [((reach, half), jnp.float32)], [held]
    )(other, columns, own)
    first = lax.axis_index("core") == 0
    ahead = lax.ppermute(jnp.where(first, samples[:EDGE], other[:EDGE]), TM, ahead_route)
    arrived = exchanged(coded(partial).reshape(near, part, half), CHAN)
    total = coded(decoded(arrived).sum(0))
    sums = exchanged(jnp.broadcast_to(total[None], (near, part, half)), CHAN)
    tail = jnp.pad(ahead, ((0, LANES - EDGE), (0, 0)))
    scale = 1.0 / (rows * groups) ** 0.5
    steps = pltpu.VMEM((cores * rows + LANES, blocks * half), jnp.bfloat16)
    (found,) = local_kernel(
        functools.partial(correlated, blocks, scale),
        [((local, blocks * half), jnp.bfloat16)],
        [pltpu.VMEM((EDGE + reach, half), jnp.float32), steps, steps],
    )(samples.T, other.T, tail.T, decoded(sums).reshape(reach, half))
    landed = exchanged(found.reshape(groups, local // groups, blocks * half), TM)
    landed = landed.reshape(groups // cores, cores, local // groups, blocks, half)
    mine = landed.astype(jnp.float32).sum(0)
    return jnp.concatenate([mine[k] for k in range(cores)], -1)[None]


def solution(mesh):
    sizes = {"y_hi": 4, "z": 8, "core": 2, "y_lo": 2, "x": 4}
    fine = Mesh(mesh.devices.reshape(tuple(sizes.values())), tuple(sizes))
    placed = (P(TM, CHAN), P(None, CHAN, None))
    return jax.shard_map(
        shards, mesh=fine, in_specs=placed, out_specs=P(CHAN, TM, None, None), check_vma=False
    )
```

```python
import functools

import jax
import jax.numpy as jnp
from jax import lax
from jax.experimental import pallas as pl
from jax.experimental.layout import Layout, with_layout_constraint
from jax.experimental.pallas import tpu as pltpu
from jax.sharding import Mesh
from jax.sharding import PartitionSpec as P


TM = ("y_hi", "z", "core")
CHAN = ("y_lo", "x")
EDGE = 8
LANES = 128
SKETCH_ROOT = 512.0
IMAGE_ROOT = 128.0
ANY = pl.BlockSpec(memory_space=pl.ANY)
VMEM = pl.BlockSpec(memory_space=pltpu.VMEM)


def local_kernel(kernel, out_shapes, scratch, in_vmem=True):
    def call(*args):
        if in_vmem:
            args = [pltpu.with_memory_space_constraint(a, pltpu.VMEM) for a in args]
        return pl.pallas_call(
            kernel,
            out_shape=[pltpu.VMEM(shape, dtype) for shape, dtype in out_shapes],
            in_specs=[VMEM if in_vmem else ANY] * len(args),
            out_specs=[VMEM] * len(out_shapes),
            scratch_shapes=scratch,
        )(*args)

    return call


def by_rows(array):
    return with_layout_constraint(array, Layout(tuple(range(array.ndim))))


def exchanged(pieces, axis):
    return lax.all_to_all(pieces, axis, split_axis=0, concat_axis=0, tiled=True)


def coded(values, root_scale):
    root = jnp.sqrt(jnp.abs(values)) * root_scale
    return jnp.where(values < 0, -root, root).astype(jnp.float16)


def decoded(codes, root_scale):
    root = codes.astype(jnp.float32) * (1.0 / root_scale)
    return root * jnp.abs(root)


def shifted_sum(held, reach, width):
    blocks = held.shape[1] // width
    total = held[EDGE : EDGE + reach, (blocks - 1) * width :]
    for j in range(blocks - 1):
        start = EDGE - (blocks - 1 - j)
        total = total + held[start : start + reach, j * width : (j + 1) * width]
    return total


def clear_edges(held, rows):
    held[:EDGE] = jnp.zeros((EDGE, held.shape[1]), jnp.float32)
    held[EDGE + rows :] = jnp.zeros((held.shape[0] - EDGE - rows, held.shape[1]), jnp.float32)


def sketched_own(samples_hbm, sketch_hbm, own_ref, columns_ref, samples_ref, held, arrivals):
    blocks = sketch_hbm.shape[0]
    rows = samples_ref.shape[0]
    reach, width = own_ref.shape
    start = pl.multiple_of(lax.axis_index("core") * width, width)
    rows_load = pltpu.make_async_copy(samples_hbm, samples_ref, arrivals.at[blocks])
    loads = [
        pltpu.make_async_copy(
            sketch_hbm.at[j, :, pl.ds(start, width)],
            columns_ref.at[:, j * width : (j + 1) * width],
            arrivals.at[j],
        )
        for j in range(blocks)
    ]
    rows_load.start()
    for load in loads:
        load.start()
    clear_edges(held, rows)
    rows_load.wait()
    for j in range(0, blocks, 2):
        pair = slice(j * width, (j + 2) * width)
        for load in loads[j : j + 2]:
            load.wait()
        held[EDGE : EDGE + rows, pair] = jnp.dot(
            samples_ref[...], columns_ref[:, pair], preferred_element_type=jnp.float32
        )
    own_ref[...] = shifted_sum(held, reach, width)


def sketched_chip(other_ref, columns_ref, own_ref, out_ref, held):
    rows = other_ref.shape[0]
    reach, width = own_ref.shape
    cores = (out_ref.shape[0] - EDGE) // rows
    clear_edges(held, rows)
    held[EDGE : EDGE + rows] = jnp.dot(
        other_ref[...], columns_ref[...], preferred_element_type=jnp.float32
    )
    core = lax.axis_index("core")
    mine = pl.ds(pl.multiple_of(core * rows, rows), reach)
    theirs = pl.ds(pl.multiple_of((cores - 1 - core) * rows, rows), reach)
    out_ref[...] = jnp.zeros_like(out_ref)
    out_ref[mine] = own_ref[...]
    out_ref[theirs] = out_ref[theirs] + shifted_sum(held, reach, width)


def correlated(block_rows, scale, own_ref, other_ref, tail_ref, sums_ref, out_ref, held, steps):
    reach, width = sums_ref.shape
    rows = own_ref.shape[1]
    cores = reach // rows
    core = lax.axis_index("core")
    mine = pl.ds(pl.multiple_of(core * rows, rows), rows)
    theirs = pl.ds(pl.multiple_of((cores - 1 - core) * rows, rows), rows)
    ends = pl.ds(cores * rows, tail_ref.shape[1])
    depth = cores * rows + 2 * EDGE
    held[:EDGE] = jnp.zeros((EDGE, width), jnp.float32)
    held[EDGE:] = sums_ref[...]
    steps[depth:] = jnp.zeros((steps.shape[0] - depth, steps.shape[1]), steps.dtype)
    for i in range(block_rows):
        moved = held[EDGE - 1 - i : EDGE - 1 - i + depth]
        steps[:depth, i * width : (i + 1) * width] = moved.astype(steps.dtype)
    wide = 2 * width
    for i in range(0, block_rows * width, wide):
        found = jnp.zeros((out_ref.shape[0], wide), jnp.float32)
        for turned, where in ((own_ref, mine), (other_ref, theirs), (tail_ref, ends)):
            found = found + jnp.dot(
                turned[...], steps[where, i : i + wide], preferred_element_type=jnp.float32
            )
        out_ref[:, i : i + wide] = found * scale


def shards(samples, sketch):
    rows, local = samples.shape
    blocks, _, width = sketch.shape
    cores = lax.axis_size("core")
    near = lax.axis_size(CHAN)
    groups = lax.axis_size(TM)
    half = width // cores
    part = -(-(cores * rows + blocks - 1) // (near * EDGE)) * EDGE
    reach = near * part
    swap = [(i, cores - 1 - i) for i in range(cores)]
    ahead_route = [(i + cores, i) for i in range(groups - cores)]

    other = by_rows(lax.ppermute(samples, "core", swap))
    held = pltpu.VMEM((rows + 3 * EDGE, blocks * half), jnp.float32)
    own, columns = local_kernel(
        sketched_own,
        [((rows + EDGE, half), jnp.float32), ((local, blocks * half), sketch.dtype)],
        [pltpu.VMEM(samples.shape, samples.dtype), held, pltpu.SemaphoreType.DMA((blocks + 1,))],
        in_vmem=False,
    )(samples, sketch)
    (partial,) = local_kernel(
        sketched_chip, [((reach, half), jnp.float32)], [held]
    )(other, columns, own)
    first = lax.axis_index("core") == 0
    ahead = lax.ppermute(jnp.where(first, samples[:EDGE], other[:EDGE]), TM, ahead_route)
    arrived = exchanged(coded(partial, SKETCH_ROOT).reshape(near, part, half), CHAN)
    total = decoded(arrived, SKETCH_ROOT).sum(0).astype(jnp.bfloat16)
    total, *turned = lax.optimization_barrier((total, samples.T, other.T))
    tail = jnp.pad(ahead, ((0, LANES - EDGE), (0, 0)))
    sums = exchanged(jnp.broadcast_to(total[None], (near, part, half)), CHAN)
    sums = sums.astype(jnp.float32).reshape(reach, half)
    scale = 1.0 / (rows * groups) ** 0.5
    (found,) = local_kernel(
        functools.partial(correlated, blocks, scale),
        [((local, blocks * half), jnp.float32)],
        [
            pltpu.VMEM((EDGE + reach, half), jnp.float32),
            pltpu.VMEM((cores * rows + LANES, blocks * half), jnp.bfloat16),
        ],
    )(*turned, tail.T, sums)
    pieces = coded(found, IMAGE_ROOT).reshape(groups, local // groups, blocks * half)
    landed = exchanged(pieces, TM)
    landed = landed.reshape(groups // cores, cores, local // groups, blocks, half)
    mine = decoded(landed, IMAGE_ROOT).sum(0)
    return jnp.concatenate([mine[k] for k in range(cores)], -1)[None]


def solution(mesh):
    sizes = {"y_hi": 4, "z": 8, "core": 2, "y_lo": 2, "x": 4}
    fine = Mesh(mesh.devices.reshape(tuple(sizes.values())), tuple(sizes))
    placed = (P(TM, CHAN), P(None, CHAN, None))
    return jax.shard_map(
        shards, mesh=fine, in_specs=placed, out_specs=P(CHAN, TM, None, None), check_vma=False
    )
```

```python
import functools

import jax
import jax.numpy as jnp
from jax import lax
from jax.experimental import pallas as pl
from jax.experimental.layout import Layout, with_layout_constraint
from jax.experimental.pallas import tpu as pltpu
from jax.sharding import Mesh
from jax.sharding import PartitionSpec as P


TM = ("y_hi", "z", "core")
CHAN = ("y_lo", "x")
EDGE = 8
LANES = 128
SKETCH_ROOT = 512.0
IMAGE_ROOT = 128.0
ANY = pl.BlockSpec(memory_space=pl.ANY)
VMEM = pl.BlockSpec(memory_space=pltpu.VMEM)


def local_kernel(kernel, out_shapes, scratch, in_vmem=True):
    def call(*args):
        if in_vmem:
            args = [pltpu.with_memory_space_constraint(a, pltpu.VMEM) for a in args]
        return pl.pallas_call(
            kernel,
            out_shape=[pltpu.VMEM(shape, dtype) for shape, dtype in out_shapes],
            in_specs=[VMEM if in_vmem else ANY] * len(args),
            out_specs=[VMEM] * len(out_shapes),
            scratch_shapes=scratch,
        )(*args)

    return call


def by_rows(array):
    return with_layout_constraint(array, Layout(tuple(range(array.ndim))))


def exchanged(pieces, axis):
    return lax.all_to_all(pieces, axis, split_axis=0, concat_axis=0, tiled=True)


def coded(values, root_scale):
    root = jnp.sqrt(jnp.abs(values)) * root_scale
    return jnp.where(values < 0, -root, root).astype(jnp.float16)


def decoded(codes, root_scale):
    root = codes.astype(jnp.float32) * (1.0 / root_scale)
    return root * jnp.abs(root)


def sketched(samples_hbm, sketch_hbm, out_ref, samples_ref, sketch_ref, held, arrivals):
    blocks = sketch_ref.shape[0]
    rows = samples_ref.shape[0]
    halves, reach, width = out_ref.shape
    own = pltpu.make_async_copy(samples_hbm, samples_ref, arrivals.at[blocks])
    loads = [
        pltpu.make_async_copy(sketch_hbm.at[j], sketch_ref.at[j], arrivals.at[j])
        for j in range(blocks)
    ]
    own.start()
    for load in loads:
        load.start()
    for j in range(blocks):
        held[j, :EDGE] = jnp.zeros((EDGE, held.shape[2]), jnp.float32)
        held[j, EDGE + rows :] = jnp.zeros((held.shape[1] - EDGE - rows, held.shape[2]), jnp.float32)
    own.wait()
    for j in range(blocks):
        loads[j].wait()
        held[j, EDGE : EDGE + rows] = jnp.dot(
            samples_ref[...], sketch_ref[j], preferred_element_type=jnp.float32
        )
    for h in range(halves):
        columns = slice(h * width, (h + 1) * width)
        total = held[blocks - 1, EDGE : EDGE + reach, columns]
        for j in range(blocks - 1):
            start = EDGE - (blocks - 1 - j)
            total = total + held[j, start : start + reach, columns]
        out_ref[h] = total


def correlated(block_rows, scale, own_ref, other_ref, tail_ref, sums_ref, out_ref, held, steps):
    parts, cores, part, width = sums_ref.shape
    rows = own_ref.shape[1]
    core = lax.axis_index("core")
    mine = pl.ds(pl.multiple_of(core * rows, rows), rows)
    theirs = pl.ds(pl.multiple_of((cores - 1 - core) * rows, rows), rows)
    ends = pl.ds(cores * rows, tail_ref.shape[1])
    depth = cores * rows + 2 * EDGE
    held[:EDGE] = jnp.zeros((EDGE, width), jnp.float32)
    held[EDGE + parts * part :] = jnp.zeros((held.shape[0] - EDGE - parts * part, width), jnp.float32)
    for k in range(cores):
        for n in range(parts):
            start = EDGE + k * rows + n * part
            there = slice(start, start + part)
            held[there] = sums_ref[n, k] if k == 0 else held[there] + sums_ref[n, k]
    steps[depth:] = jnp.zeros((steps.shape[0] - depth, steps.shape[1]), steps.dtype)
    for i in range(block_rows):
        moved = held[EDGE - 1 - i : EDGE - 1 - i + depth]
        steps[:depth, i * width : (i + 1) * width] = moved.astype(steps.dtype)
    wide = 2 * width
    for i in range(0, block_rows * width, wide):
        found = jnp.zeros((out_ref.shape[0], wide), jnp.float32)
        for turned, where in ((own_ref, mine), (other_ref, theirs), (tail_ref, ends)):
            found = found + jnp.dot(
                turned[...], steps[where, i : i + wide], preferred_element_type=jnp.float32
            )
        out_ref[:, i : i + wide] = found * scale


def shards(samples, sketch):
    rows, local = samples.shape
    blocks, _, width = sketch.shape
    cores = lax.axis_size("core")
    near = lax.axis_size(CHAN)
    groups = lax.axis_size(TM)
    half = width // cores
    part = -(-(rows + blocks - 1) // (near * EDGE)) * EDGE
    reach = near * part
    swap = [(i, cores - 1 - i) for i in range(cores)]
    chips = range(0, groups - cores, cores)

    (partial,) = local_kernel(
        sketched,
        [((cores, reach, half), jnp.float32)],
        [
            pltpu.VMEM(samples.shape, samples.dtype),
            pltpu.VMEM(sketch.shape, sketch.dtype),
            pltpu.VMEM((blocks, reach + 2 * EDGE, width), jnp.float32),
            pltpu.SemaphoreType.DMA((blocks + 1,)),
        ],
        in_vmem=False,
    )(samples, sketch)
    pieces = coded(partial, SKETCH_ROOT).reshape(cores * near, part, half)
    arrived = exchanged(pieces, ("core", *CHAN)).reshape(cores, near, part, half)
    other = by_rows(lax.ppermute(samples, "core", swap))
    heads = []
    for core in range(cores):
        route = [(i + cores, i + core) for i in chips]
        heads.append(lax.ppermute(samples[:EDGE], TM, route))
    ahead = sum(heads[1:], heads[0])
    total = decoded(arrived, SKETCH_ROOT).sum(1).astype(jnp.bfloat16)
    total = total.reshape(cores * part, half)
    total, *turned = lax.optimization_barrier((total, samples.T, other.T))
    tail = jnp.pad(ahead, ((0, LANES - EDGE), (0, 0)))
    sums = exchanged(jnp.broadcast_to(total[None], (near, cores * part, half)), CHAN)
    sums = sums.astype(jnp.float32).reshape(near, cores, part, half)
    scale = 1.0 / (rows * groups) ** 0.5
    (found,) = local_kernel(
        functools.partial(correlated, blocks, scale),
        [((local, blocks * half), jnp.float32)],
        [
            pltpu.VMEM((EDGE + (cores - 1) * rows + reach, half), jnp.float32),
            pltpu.VMEM((cores * rows + LANES, blocks * half), jnp.bfloat16),
        ],
    )(*turned, tail.T, sums)
    pieces = coded(found, IMAGE_ROOT).reshape(groups, local // groups, blocks * half)
    landed = exchanged(pieces, TM)
    landed = landed.reshape(groups // cores, cores, local // groups, blocks, half)
    mine = decoded(landed, IMAGE_ROOT).sum(0)
    return jnp.concatenate([mine[k] for k in range(cores)], -1)[None]


def solution(mesh):
    sizes = {"y_hi": 4, "z": 8, "core": 2, "y_lo": 2, "x": 4}
    fine = Mesh(mesh.devices.reshape(tuple(sizes.values())), tuple(sizes))
    placed = (P(TM, CHAN), P(None, CHAN, None))
    return jax.shard_map(shards, mesh=fine, in_specs=placed, out_specs=P(CHAN, TM, None, None), check_vma=False)
```

```python
import functools

import jax
import jax.numpy as jnp
from jax import lax
from jax.experimental import pallas as pl
from jax.experimental.layout import Layout, with_layout_constraint
from jax.experimental.pallas import tpu as pltpu
from jax.sharding import Mesh
from jax.sharding import PartitionSpec as P


TM = ("y_hi", "z", "core")
CHAN = ("y_lo", "x")
EDGE = 8
LANES = 128
SKETCH_ROOT = 512.0
IMAGE_ROOT = 128.0
ANY = pl.BlockSpec(memory_space=pl.ANY)
VMEM = pl.BlockSpec(memory_space=pltpu.VMEM)


def local_kernel(kernel, out_shapes, scratch, in_vmem=True):
    def call(*args):
        if in_vmem:
            args = [pltpu.with_memory_space_constraint(a, pltpu.VMEM) for a in args]
        return pl.pallas_call(
            kernel,
            out_shape=[pltpu.VMEM(shape, dtype) for shape, dtype in out_shapes],
            in_specs=[VMEM if in_vmem else ANY] * len(args),
            out_specs=[VMEM] * len(out_shapes),
            scratch_shapes=scratch,
        )(*args)

    return call


def by_rows(array):
    return with_layout_constraint(array, Layout(tuple(range(array.ndim))))


def exchanged(pieces, axis):
    return lax.all_to_all(pieces, axis, split_axis=0, concat_axis=0, tiled=True)


def coded(values, root_scale):
    root = jnp.sqrt(jnp.abs(values)) * root_scale
    return jnp.where(values < 0, -root, root).astype(jnp.float16)


def decoded(codes, root_scale):
    root = codes.astype(jnp.float32) * (1.0 / root_scale)
    return root * jnp.abs(root)


def shifted_sum(held, first, reach, width):
    blocks = held.shape[1] // width
    total = held[EDGE + first : EDGE + first + reach, (blocks - 1) * width :]
    for j in range(blocks - 1):
        start = EDGE + first - (blocks - 1 - j)
        total = total + held[start : start + reach, j * width : (j + 1) * width]
    return total


def clear_edges(held, rows):
    held[:EDGE] = jnp.zeros((EDGE, held.shape[1]), jnp.float32)
    held[EDGE + rows :] = jnp.zeros((held.shape[0] - EDGE - rows, held.shape[1]), jnp.float32)


def sketched_own(samples_hbm, sketch_hbm, own_ref, columns_ref, samples_ref, held, arrivals):
    blocks = sketch_hbm.shape[0]
    rows = samples_ref.shape[0]
    reach, width = own_ref.shape
    start = pl.multiple_of(lax.axis_index("core") * width, width)
    step = rows // 2
    rows_loads = [
        pltpu.make_async_copy(
            samples_hbm.at[n : n + step], samples_ref.at[n : n + step], arrivals.at[blocks + n // step]
        )
        for n in range(0, rows, step)
    ]
    loads = [
        pltpu.make_async_copy(
            sketch_hbm.at[j, :, pl.ds(start, width)],
            columns_ref.at[:, j * width : (j + 1) * width],
            arrivals.at[j],
        )
        for j in range(blocks)
    ]
    rows_loads[0].start()
    for load in loads + rows_loads[1:]:
        load.start()
    clear_edges(held, rows)
    for load in loads:
        load.wait()
    for n, load in zip(range(0, rows, step), rows_loads):
        load.wait()
        held[EDGE + n : EDGE + n + step] = jnp.dot(
            samples_ref[n : n + step], columns_ref[...], preferred_element_type=jnp.float32
        )
        end = n + step if n + step < rows else reach
        own_ref[n:end] = shifted_sum(held, n, end - n, width)


def sketched_chip(other_ref, columns_ref, own_ref, out_ref, held):
    rows = other_ref.shape[0]
    reach, width = own_ref.shape
    cores = (out_ref.shape[0] - EDGE) // rows
    clear_edges(held, rows)
    held[EDGE : EDGE + rows] = jnp.dot(
        other_ref[...], columns_ref[...], preferred_element_type=jnp.float32
    )
    core = lax.axis_index("core")
    mine = pl.ds(pl.multiple_of(core * rows, rows), reach)
    theirs = pl.ds(pl.multiple_of((cores - 1 - core) * rows, rows), reach)
    out_ref[...] = jnp.zeros_like(out_ref)
    out_ref[mine] = own_ref[...]
    out_ref[theirs] = out_ref[theirs] + shifted_sum(held, 0, reach, width)


def correlated(block_rows, scale, own_ref, other_ref, tail_ref, sums_ref, out_ref, held, steps):
    reach, width = sums_ref.shape
    rows = own_ref.shape[1]
    cores = reach // rows
    core = lax.axis_index("core")
    mine = pl.ds(pl.multiple_of(core * rows, rows), rows)
    theirs = pl.ds(pl.multiple_of((cores - 1 - core) * rows, rows), rows)
    ends = pl.ds(cores * rows, tail_ref.shape[1])
    depth = cores * rows + 2 * EDGE
    held[:EDGE] = jnp.zeros((EDGE, width), jnp.float32)
    held[EDGE:] = sums_ref[...]
    steps[depth:] = jnp.zeros((steps.shape[0] - depth, steps.shape[1]), steps.dtype)
    for i in range(block_rows):
        moved = held[EDGE - 1 - i : EDGE - 1 - i + depth]
        steps[:depth, i * width : (i + 1) * width] = moved.astype(steps.dtype)
    wide = 2 * width
    for i in range(0, block_rows * width, wide):
        found = jnp.zeros((out_ref.shape[0], wide), jnp.float32)
        for turned, where in ((own_ref, mine), (other_ref, theirs), (tail_ref, ends)):
            found = found + jnp.dot(
                turned[...], steps[where, i : i + wide], preferred_element_type=jnp.float32
            )
        out_ref[:, i : i + wide] = found * scale


def shards(samples, sketch):
    rows, local = samples.shape
    blocks, _, width = sketch.shape
    cores = lax.axis_size("core")
    near = lax.axis_size(CHAN)
    groups = lax.axis_size(TM)
    half = width // cores
    part = -(-(cores * rows + blocks - 1) // (near * EDGE)) * EDGE
    reach = near * part
    swap = [(i, cores - 1 - i) for i in range(cores)]
    ahead_route = [(i + cores, i) for i in range(groups - cores)]

    other = by_rows(lax.ppermute(samples, "core", swap))
    held = pltpu.VMEM((rows + 3 * EDGE, blocks * half), jnp.float32)
    own, columns = local_kernel(
        sketched_own,
        [((rows + EDGE, half), jnp.float32), ((local, blocks * half), sketch.dtype)],
        [pltpu.VMEM(samples.shape, samples.dtype), held, pltpu.SemaphoreType.DMA((blocks + 2,))],
        in_vmem=False,
    )(samples, sketch)
    (partial,) = local_kernel(sketched_chip, [((reach, half), jnp.float32)], [held])(other, columns, own)
    first = lax.axis_index("core") == 0
    ahead = lax.ppermute(jnp.where(first, samples[:EDGE], other[:EDGE]), TM, ahead_route)
    arrived = exchanged(coded(partial, SKETCH_ROOT).reshape(near, part, half), CHAN)
    total = decoded(arrived, SKETCH_ROOT).sum(0).astype(jnp.bfloat16)
    total, *turned = lax.optimization_barrier((total, samples.T, other.T))
    tail = jnp.pad(ahead, ((0, LANES - EDGE), (0, 0)))
    sums = exchanged(jnp.broadcast_to(total[None], (near, part, half)), CHAN)
    sums = sums.astype(jnp.float32).reshape(reach, half)
    scale = 1.0 / (rows * groups) ** 0.5
    (found,) = local_kernel(
        functools.partial(correlated, blocks, scale),
        [((local, blocks * half), jnp.float32)],
        [
            pltpu.VMEM((EDGE + reach, half), jnp.float32),
            pltpu.VMEM((cores * rows + LANES, blocks * half), jnp.bfloat16),
        ],
    )(*turned, tail.T, sums)
    pieces = coded(found, IMAGE_ROOT).reshape(groups, local // groups, blocks * half)
    landed = exchanged(pieces, TM)
    landed = landed.reshape(groups // cores, cores, local // groups, blocks * half)
    mine = decoded(landed, IMAGE_ROOT).sum(0).reshape(cores, local // groups, blocks, half)
    return jnp.concatenate([mine[k] for k in range(cores)], -1)[None]


def solution(mesh):
    sizes = {"y_hi": 4, "z": 8, "core": 2, "y_lo": 2, "x": 4}
    fine = Mesh(mesh.devices.reshape(tuple(sizes.values())), tuple(sizes))
    placed = (P(TM, CHAN), P(None, CHAN, None))
    return jax.shard_map(shards, mesh=fine, in_specs=placed, out_specs=P(CHAN, TM, None, None), check_vma=False)
```

```python
import functools

import jax
import jax.numpy as jnp
from jax import lax
from jax.experimental import pallas as pl
from jax.experimental.layout import Layout, with_layout_constraint
from jax.experimental.pallas import tpu as pltpu
from jax.sharding import Mesh
from jax.sharding import PartitionSpec as P


TM = ("y_hi", "z", "core")
CHAN = ("y_lo", "x")
EDGE = 8
LANES = 128
SKETCH_ROOT = 512.0
IMAGE_ROOT = 128.0
ANY = pl.BlockSpec(memory_space=pl.ANY)
VMEM = pl.BlockSpec(memory_space=pltpu.VMEM)


def local_kernel(kernel, out_shapes, scratch, in_vmem=True):
    def call(*args):
        if in_vmem:
            args = [pltpu.with_memory_space_constraint(a, pltpu.VMEM) for a in args]
        return pl.pallas_call(
            kernel,
            out_shape=[pltpu.VMEM(shape, dtype) for shape, dtype in out_shapes],
            in_specs=[VMEM if in_vmem else ANY] * len(args),
            out_specs=[VMEM] * len(out_shapes),
            scratch_shapes=scratch,
        )(*args)

    return call


def by_rows(array):
    return with_layout_constraint(array, Layout(tuple(range(array.ndim))))


def exchanged(pieces, axis):
    return lax.all_to_all(pieces, axis, split_axis=0, concat_axis=0, tiled=True)


def rooted(values, root_scale):
    root = jnp.sqrt(jnp.abs(values)) * root_scale
    return jnp.where(values < 0, -root, root)


def squared(codes, root_scale):
    root = codes.astype(jnp.float32)
    square = root * root
    return jnp.where(root < 0, -square, square) * (1.0 / root_scale**2)


def shifted_sum(held, first, reach, width):
    blocks = held.shape[1] // width
    total = held[EDGE + first : EDGE + first + reach, (blocks - 1) * width :]
    for j in range(blocks - 1):
        start = EDGE + first - (blocks - 1 - j)
        total = total + held[start : start + reach, j * width : (j + 1) * width]
    return total


def clear_edges(held, rows):
    held[:EDGE] = jnp.zeros((EDGE, held.shape[1]), jnp.float32)
    held[EDGE + rows :] = jnp.zeros((held.shape[0] - EDGE - rows, held.shape[1]), jnp.float32)


def sketched_own(samples_hbm, sketch_hbm, own_ref, columns_ref, samples_ref, held, arrivals):
    blocks = sketch_hbm.shape[0]
    rows = samples_ref.shape[0]
    reach, width = own_ref.shape
    start = pl.multiple_of(lax.axis_index("core") * width, width)
    step = rows // 2
    rows_loads = [
        pltpu.make_async_copy(
            samples_hbm.at[n : n + step], samples_ref.at[n : n + step], arrivals.at[blocks + n // step]
        )
        for n in range(0, rows, step)
    ]
    loads = [
        pltpu.make_async_copy(
            sketch_hbm.at[j, :, pl.ds(start, width)],
            columns_ref.at[:, j * width : (j + 1) * width],
            arrivals.at[j],
        )
        for j in range(blocks)
    ]
    rows_loads[0].start()
    for load in loads + rows_loads[1:]:
        load.start()
    clear_edges(held, rows)
    for load in loads:
        load.wait()
    for n, load in zip(range(0, rows, step), rows_loads):
        load.wait()
        held[EDGE + n : EDGE + n + step] = jnp.dot(
            samples_ref[n : n + step], columns_ref[...], preferred_element_type=jnp.float32
        )
        end = n + step if n + step < rows else reach
        own_ref[n:end] = shifted_sum(held, n, end - n, width)


def sketched_chip(other_ref, columns_ref, own_ref, out_ref, held):
    rows = other_ref.shape[0]
    reach, width = own_ref.shape
    cores = (out_ref.shape[0] - EDGE) // rows
    clear_edges(held, rows)
    held[EDGE : EDGE + rows] = jnp.dot(
        other_ref[...], columns_ref[...], preferred_element_type=jnp.float32
    )
    core = lax.axis_index("core")
    mine = pl.ds(pl.multiple_of(core * rows, rows), reach)
    theirs = pl.ds(pl.multiple_of((cores - 1 - core) * rows, rows), reach)
    out_ref[...] = jnp.zeros_like(out_ref)
    out_ref[mine] = own_ref[...]
    out_ref[theirs] = out_ref[theirs] + shifted_sum(held, 0, reach, width)
    out_ref[...] = rooted(out_ref[...], SKETCH_ROOT)


def correlated(block_rows, scale, own_ref, other_ref, tail_ref, sums_ref, out_ref, held, steps):
    reach, width = sums_ref.shape
    rows = own_ref.shape[1]
    cores = reach // rows
    core = lax.axis_index("core")
    mine = pl.ds(pl.multiple_of(core * rows, rows), rows)
    theirs = pl.ds(pl.multiple_of((cores - 1 - core) * rows, rows), rows)
    ends = pl.ds(cores * rows, tail_ref.shape[1])
    depth = cores * rows + 2 * EDGE
    held[:EDGE] = jnp.zeros((EDGE, width), jnp.float32)
    held[EDGE:] = sums_ref[...]
    steps[depth:] = jnp.zeros((steps.shape[0] - depth, steps.shape[1]), steps.dtype)
    for i in range(block_rows):
        moved = held[EDGE - 1 - i : EDGE - 1 - i + depth]
        steps[:depth, i * width : (i + 1) * width] = moved.astype(steps.dtype)
    wide = 2 * width
    for i in range(0, block_rows * width, wide):
        found = jnp.zeros((out_ref.shape[0], wide), jnp.float32)
        for turned, where in ((own_ref, mine), (other_ref, theirs), (tail_ref, ends)):
            found = found + jnp.dot(
                turned[...], steps[where, i : i + wide], preferred_element_type=jnp.float32
            )
        out_ref[:, i : i + wide] = rooted(found * scale, IMAGE_ROOT)


def shards(samples, sketch):
    rows, local = samples.shape
    blocks, _, width = sketch.shape
    cores = lax.axis_size("core")
    near = lax.axis_size(CHAN)
    groups = lax.axis_size(TM)
    half = width // cores
    part = -(-(cores * rows + blocks - 1) // (near * EDGE)) * EDGE
    reach = near * part
    swap = [(i, cores - 1 - i) for i in range(cores)]
    ahead_route = [(i + cores, i) for i in range(groups - cores)]

    other = by_rows(lax.ppermute(samples, "core", swap))
    held = pltpu.VMEM((rows + 3 * EDGE, blocks * half), jnp.float32)
    own, columns = local_kernel(
        sketched_own,
        [((rows + EDGE, half), jnp.float32), ((local, blocks * half), sketch.dtype)],
        [pltpu.VMEM(samples.shape, samples.dtype), held, pltpu.SemaphoreType.DMA((blocks + 2,))],
        in_vmem=False,
    )(samples, sketch)
    (partial,) = local_kernel(sketched_chip, [((reach, half), jnp.float32)], [held])(other, columns, own)
    first = lax.axis_index("core") == 0
    ahead = lax.ppermute(jnp.where(first, samples[:EDGE], other[:EDGE]), TM, ahead_route)
    arrived = exchanged(partial.astype(jnp.float16).reshape(near, part, half), CHAN)
    total = squared(arrived, SKETCH_ROOT).sum(0).astype(jnp.bfloat16)
    total, *turned = lax.optimization_barrier((total, samples.T, other.T))
    tail = jnp.pad(ahead, ((0, LANES - EDGE), (0, 0)))
    sums = exchanged(jnp.broadcast_to(total[None], (near, part, half)), CHAN)
    sums = sums.astype(jnp.float32).reshape(reach, half)
    scale = 1.0 / (rows * groups) ** 0.5
    (found,) = local_kernel(
        functools.partial(correlated, blocks, scale),
        [((local, blocks * half), jnp.float32)],
        [
            pltpu.VMEM((EDGE + reach, half), jnp.float32),
            pltpu.VMEM((cores * rows + LANES, blocks * half), jnp.bfloat16),
        ],
    )(*turned, tail.T, sums)
    pieces = found.astype(jnp.float16).reshape(groups, local // groups, blocks * half)
    landed = exchanged(pieces, TM)
    landed = landed.reshape(groups // cores, cores, local // groups, blocks * half)
    landed = lax.optimization_barrier(landed)
    mine = squared(landed, IMAGE_ROOT).sum(0).reshape(cores, local // groups, blocks, half)
    return jnp.concatenate([mine[k] for k in range(cores)], -1)[None]


def solution(mesh):
    sizes = {"y_hi": 4, "z": 8, "core": 2, "y_lo": 2, "x": 4}
    fine = Mesh(mesh.devices.reshape(tuple(sizes.values())), tuple(sizes))
    placed = (P(TM, CHAN), P(None, CHAN, None))
    return jax.shard_map(shards, mesh=fine, in_specs=placed, out_specs=P(CHAN, TM, None, None), check_vma=False)
```

```python
import functools

import jax
import jax.numpy as jnp
from jax import lax
from jax.experimental import pallas as pl
from jax.experimental.layout import Layout, with_layout_constraint
from jax.experimental.pallas import tpu as pltpu
from jax.sharding import Mesh
from jax.sharding import PartitionSpec as P


TM = ("y_hi", "z", "core")
CHAN = ("y_lo", "x")
EDGE = 8
LANES = 128
SKETCH_ROOT = 512.0
IMAGE_ROOT = 128.0
LEAST = 1e-30
ANY = pl.BlockSpec(memory_space=pl.ANY)
VMEM = pl.BlockSpec(memory_space=pltpu.VMEM)


def local_kernel(kernel, out_shapes, scratch, in_vmem=True):
    def call(*args):
        if in_vmem:
            args = [pltpu.with_memory_space_constraint(a, pltpu.VMEM) for a in args]
        return pl.pallas_call(
            kernel,
            out_shape=[pltpu.VMEM(shape, dtype) for shape, dtype in out_shapes],
            in_specs=[VMEM if in_vmem else ANY] * len(args),
            out_specs=[VMEM] * len(out_shapes),
            scratch_shapes=scratch,
        )(*args)

    return call


def by_rows(array):
    return with_layout_constraint(array, Layout(tuple(range(array.ndim))))


def exchanged(pieces, axis):
    return lax.all_to_all(pieces, axis, split_axis=0, concat_axis=0, tiled=True)


def coded(values, root_scale):
    root = values * lax.rsqrt(jnp.maximum(jnp.abs(values), LEAST))
    return (root * root_scale).astype(jnp.float16)


def decoded(codes, root_scale):
    root = codes.astype(jnp.float32) * (1.0 / root_scale)
    return root * jnp.abs(root)


def shifted_sum(held, first, reach, width):
    blocks = held.shape[1] // width
    total = held[EDGE + first : EDGE + first + reach, (blocks - 1) * width :]
    for j in range(blocks - 1):
        start = EDGE + first - (blocks - 1 - j)
        total = total + held[start : start + reach, j * width : (j + 1) * width]
    return total


def clear_edges(held, rows):
    held[:EDGE] = jnp.zeros((EDGE, held.shape[1]), jnp.float32)
    held[EDGE + rows :] = jnp.zeros((held.shape[0] - EDGE - rows, held.shape[1]), jnp.float32)


def sketched_own(samples_hbm, sketch_hbm, own_ref, columns_ref, samples_ref, held, arrivals):
    blocks = sketch_hbm.shape[0]
    rows = samples_ref.shape[0]
    reach, width = own_ref.shape
    start = pl.multiple_of(lax.axis_index("core") * width, width)
    step = rows // 2
    rows_loads = [
        pltpu.make_async_copy(
            samples_hbm.at[n : n + step], samples_ref.at[n : n + step], arrivals.at[blocks + n // step]
        )
        for n in range(0, rows, step)
    ]
    loads = [
        pltpu.make_async_copy(
            sketch_hbm.at[j, :, pl.ds(start, width)],
            columns_ref.at[:, j * width : (j + 1) * width],
            arrivals.at[j],
        )
        for j in range(blocks)
    ]
    rows_loads[0].start()
    for load in loads + rows_loads[1:]:
        load.start()
    clear_edges(held, rows)
    for load in loads:
        load.wait()
    for n, load in zip(range(0, rows, step), rows_loads):
        load.wait()
        held[EDGE + n : EDGE + n + step] = jnp.dot(
            samples_ref[n : n + step], columns_ref[...], preferred_element_type=jnp.float32
        )
        end = n + step if n + step < rows else reach
        own_ref[n:end] = shifted_sum(held, n, end - n, width)


def sketched_chip(other_ref, columns_ref, own_ref, out_ref, held):
    rows = other_ref.shape[0]
    reach, width = own_ref.shape
    cores = (out_ref.shape[0] - EDGE) // rows
    clear_edges(held, rows)
    held[EDGE : EDGE + rows] = jnp.dot(
        other_ref[...], columns_ref[...], preferred_element_type=jnp.float32
    )
    core = lax.axis_index("core")
    mine = pl.ds(pl.multiple_of(core * rows, rows), reach)
    theirs = pl.ds(pl.multiple_of((cores - 1 - core) * rows, rows), reach)
    out_ref[...] = jnp.zeros_like(out_ref)
    out_ref[mine] = own_ref[...]
    out_ref[theirs] = out_ref[theirs] + shifted_sum(held, 0, reach, width)


def correlated(block_rows, scale, own_ref, other_ref, tail_ref, sums_ref, out_ref, held, steps):
    reach, width = sums_ref.shape
    rows = own_ref.shape[1]
    cores = reach // rows
    core = lax.axis_index("core")
    mine = pl.ds(pl.multiple_of(core * rows, rows), rows)
    theirs = pl.ds(pl.multiple_of((cores - 1 - core) * rows, rows), rows)
    ends = pl.ds(cores * rows, tail_ref.shape[1])
    depth = cores * rows + 2 * EDGE
    held[:EDGE] = jnp.zeros((EDGE, width), jnp.float32)
    held[EDGE:] = sums_ref[...]
    steps[depth:] = jnp.zeros((steps.shape[0] - depth, steps.shape[1]), steps.dtype)
    for i in range(block_rows):
        moved = held[EDGE - 1 - i : EDGE - 1 - i + depth]
        steps[:depth, i * width : (i + 1) * width] = moved.astype(steps.dtype)
    wide = 2 * width
    for i in range(0, block_rows * width, wide):
        found = jnp.zeros((out_ref.shape[0], wide), jnp.float32)
        for turned, where in ((own_ref, mine), (other_ref, theirs), (tail_ref, ends)):
            found = found + jnp.dot(
                turned[...], steps[where, i : i + wide], preferred_element_type=jnp.float32
            )
        out_ref[:, i : i + wide] = found * scale


def shards(samples, sketch):
    rows, local = samples.shape
    blocks, _, width = sketch.shape
    cores = lax.axis_size("core")
    near = lax.axis_size(CHAN)
    groups = lax.axis_size(TM)
    half = width // cores
    part = -(-(cores * rows + blocks - 1) // (near * EDGE)) * EDGE
    reach = near * part
    swap = [(i, cores - 1 - i) for i in range(cores)]
    ahead_route = [(i + cores, i) for i in range(groups - cores)]

    other = by_rows(lax.ppermute(samples, "core", swap))
    held = pltpu.VMEM((rows + 3 * EDGE, blocks * half), jnp.float32)
    own, columns = local_kernel(
        sketched_own,
        [((rows + EDGE, half), jnp.float32), ((local, blocks * half), sketch.dtype)],
        [pltpu.VMEM(samples.shape, samples.dtype), held, pltpu.SemaphoreType.DMA((blocks + 2,))],
        in_vmem=False,
    )(samples, sketch)
    (partial,) = local_kernel(sketched_chip, [((reach, half), jnp.float32)], [held])(other, columns, own)
    first = lax.axis_index("core") == 0
    ahead = lax.ppermute(jnp.where(first, samples[:EDGE], other[:EDGE]), TM, ahead_route)
    arrived = exchanged(coded(partial, SKETCH_ROOT).reshape(near, part, half), CHAN)
    total = decoded(arrived, SKETCH_ROOT).sum(0).astype(jnp.bfloat16)
    total, *turned = lax.optimization_barrier((total, samples.T, other.T))
    tail = jnp.pad(ahead, ((0, LANES - EDGE), (0, 0)))
    sums = exchanged(jnp.broadcast_to(total[None], (near, part, half)), CHAN)
    sums = sums.astype(jnp.float32).reshape(reach, half)
    scale = 1.0 / (rows * groups) ** 0.5
    (found,) = local_kernel(
        functools.partial(correlated, blocks, scale),
        [((local, blocks * half), jnp.float32)],
        [
            pltpu.VMEM((EDGE + reach, half), jnp.float32),
            pltpu.VMEM((cores * rows + LANES, blocks * half), jnp.bfloat16),
        ],
    )(*turned, tail.T, sums)
    pieces = coded(found, IMAGE_ROOT).reshape(groups, local // groups, blocks * half)
    landed = exchanged(pieces, TM)
    landed = landed.reshape(groups // cores, cores, local // groups, blocks * half)
    landed = lax.optimization_barrier(landed)
    mine = decoded(landed, IMAGE_ROOT).sum(0).reshape(cores, local // groups, blocks, half)
    return jnp.concatenate([mine[k] for k in range(cores)], -1)[None]


def solution(mesh):
    sizes = {"y_hi": 4, "z": 8, "core": 2, "y_lo": 2, "x": 4}
    fine = Mesh(mesh.devices.reshape(tuple(sizes.values())), tuple(sizes))
    placed = (P(TM, CHAN), P(None, CHAN, None))
    return jax.shard_map(shards, mesh=fine, in_specs=placed, out_specs=P(CHAN, TM, None, None), check_vma=False)
```

```python
import functools

import jax
import jax.numpy as jnp
from jax import lax
from jax.experimental import pallas as pl
from jax.experimental.layout import Layout, with_layout_constraint
from jax.experimental.pallas import tpu as pltpu
from jax.sharding import Mesh
from jax.sharding import PartitionSpec as P


TM = ("y_hi", "z", "core")
CHAN = ("y_lo", "x")
EDGE = 8
SKETCH_ROOT = 512.0
IMAGE_ROOT = 128.0
LEAST = 1e-30
ANY = pl.BlockSpec(memory_space=pl.ANY)
VMEM = pl.BlockSpec(memory_space=pltpu.VMEM)


def local_kernel(kernel, out_shapes, scratch, in_vmem=True):
    def call(*args):
        if in_vmem:
            args = [pltpu.with_memory_space_constraint(a, pltpu.VMEM) for a in args]
        return pl.pallas_call(
            kernel,
            out_shape=[pltpu.VMEM(shape, dtype) for shape, dtype in out_shapes],
            in_specs=[VMEM if in_vmem else ANY] * len(args),
            out_specs=[VMEM] * len(out_shapes),
            scratch_shapes=scratch,
        )(*args)

    return call


def by_rows(array):
    return with_layout_constraint(array, Layout(tuple(range(array.ndim))))


def exchanged(pieces, axis):
    return lax.all_to_all(pieces, axis, split_axis=0, concat_axis=0, tiled=True)


def coded(values, root_scale):
    root = values * lax.rsqrt(jnp.maximum(jnp.abs(values), LEAST))
    return (root * root_scale).astype(jnp.float16)


def decoded(codes, root_scale):
    root = codes.astype(jnp.float32) * (1.0 / root_scale)
    return root * jnp.abs(root)


def shifted_sum(held, first, reach, width):
    blocks = held.shape[1] // width
    total = held[EDGE + first : EDGE + first + reach, (blocks - 1) * width :]
    for j in range(blocks - 1):
        start = EDGE + first - (blocks - 1 - j)
        total = total + held[start : start + reach, j * width : (j + 1) * width]
    return total


def clear_edges(held, rows):
    held[:EDGE] = jnp.zeros((EDGE, held.shape[1]), jnp.float32)
    held[EDGE + rows :] = jnp.zeros((held.shape[0] - EDGE - rows, held.shape[1]), jnp.float32)


def sketched_own(samples_hbm, sketch_hbm, own_ref, columns_ref, samples_ref, held, arrivals):
    blocks = sketch_hbm.shape[0]
    rows = samples_ref.shape[0]
    reach, width = own_ref.shape
    start = pl.multiple_of(lax.axis_index("core") * width, width)
    step = rows // 2
    rows_loads = [
        pltpu.make_async_copy(
            samples_hbm.at[n : n + step], samples_ref.at[n : n + step], arrivals.at[blocks + n // step]
        )
        for n in range(0, rows, step)
    ]
    loads = [
        pltpu.make_async_copy(
            sketch_hbm.at[j, :, pl.ds(start, width)],
            columns_ref.at[:, j * width : (j + 1) * width],
            arrivals.at[j],
        )
        for j in range(blocks)
    ]
    rows_loads[0].start()
    for load in loads + rows_loads[1:]:
        load.start()
    clear_edges(held, rows)
    for load in loads:
        load.wait()
    for n, load in zip(range(0, rows, step), rows_loads):
        load.wait()
        held[EDGE + n : EDGE + n + step] = jnp.dot(
            samples_ref[n : n + step], columns_ref[...], preferred_element_type=jnp.float32
        )
        end = n + step if n + step < rows else reach
        own_ref[n:end] = shifted_sum(held, n, end - n, width)


def sketched_chip(other_ref, columns_ref, own_ref, out_ref, held):
    rows = other_ref.shape[0]
    reach, width = own_ref.shape
    cores = (out_ref.shape[0] - EDGE) // rows
    clear_edges(held, rows)
    held[EDGE : EDGE + rows] = jnp.dot(
        other_ref[...], columns_ref[...], preferred_element_type=jnp.float32
    )
    core = lax.axis_index("core")
    mine = pl.ds(pl.multiple_of(core * rows, rows), reach)
    theirs = pl.ds(pl.multiple_of((cores - 1 - core) * rows, rows), reach)
    out_ref[...] = jnp.zeros_like(out_ref)
    out_ref[mine] = own_ref[...]
    out_ref[theirs] = out_ref[theirs] + shifted_sum(held, 0, reach, width)


def correlated(block_rows, scale, own_ref, other_ref, tail_ref, sums_ref, out_ref, held, steps):
    reach, width = sums_ref.shape
    rows = own_ref.shape[1]
    cores = reach // rows
    core = lax.axis_index("core")
    mine = pl.ds(pl.multiple_of(core * rows, rows), rows)
    theirs = pl.ds(pl.multiple_of((cores - 1 - core) * rows, rows), rows)
    ends = pl.ds(cores * rows, tail_ref.shape[0])
    depth = cores * rows + 2 * EDGE
    held[:EDGE] = jnp.zeros((EDGE, width), jnp.float32)
    held[EDGE:] = sums_ref[...]
    for i in range(block_rows):
        moved = held[EDGE - 1 - i : EDGE - 1 - i + depth]
        steps[:depth, i * width : (i + 1) * width] = moved.astype(steps.dtype)
    wide = 2 * width
    for i in range(0, block_rows * width, wide):
        found = lax.dot_general(
            tail_ref[...],
            steps[ends, i : i + wide],
            (((0,), (0,)), ((), ())),
            preferred_element_type=jnp.float32,
        )
        for turned, where in ((own_ref, mine), (other_ref, theirs)):
            found = found + jnp.dot(
                turned[...], steps[where, i : i + wide], preferred_element_type=jnp.float32
            )
        out_ref[:, i : i + wide] = found * scale


def shards(samples, sketch):
    rows, local = samples.shape
    blocks, _, width = sketch.shape
    cores = lax.axis_size("core")
    near = lax.axis_size(CHAN)
    groups = lax.axis_size(TM)
    half = width // cores
    part = -(-(cores * rows + blocks - 1) // (near * EDGE)) * EDGE
    reach = near * part
    swap = [(i, cores - 1 - i) for i in range(cores)]
    ahead_route = [(i + cores, i) for i in range(groups - cores)]

    other = by_rows(lax.ppermute(samples, "core", swap))
    held = pltpu.VMEM((rows + 3 * EDGE, blocks * half), jnp.float32)
    own, columns = local_kernel(
        sketched_own,
        [((rows + EDGE, half), jnp.float32), ((local, blocks * half), sketch.dtype)],
        [pltpu.VMEM(samples.shape, samples.dtype), held, pltpu.SemaphoreType.DMA((blocks + 2,))],
        in_vmem=False,
    )(samples, sketch)
    (partial,) = local_kernel(
        sketched_chip, [((reach, half), jnp.float32)], [held]
    )(other, columns, own)
    first = lax.axis_index("core") == 0
    edge = jnp.where(first, samples[:EDGE], other[:EDGE])
    ahead = by_rows(lax.ppermute(edge, TM, ahead_route))
    arrived = exchanged(coded(partial, SKETCH_ROOT).reshape(near, part, half), CHAN)
    total = decoded(arrived, SKETCH_ROOT).sum(0).astype(jnp.bfloat16)
    total, *turned = lax.optimization_barrier((total, samples.T, other.T))
    tail = jnp.pad(ahead, ((0, EDGE), (0, 0)))
    sums = exchanged(jnp.broadcast_to(total[None], (near, part, half)), CHAN)
    sums = sums.astype(jnp.float32).reshape(reach, half)
    scale = 1.0 / (rows * groups) ** 0.5
    (found,) = local_kernel(
        functools.partial(correlated, blocks, scale),
        [((local, blocks * half), jnp.float32)],
        [
            pltpu.VMEM((EDGE + reach, half), jnp.float32),
            pltpu.VMEM((cores * rows + 2 * EDGE, blocks * half), jnp.bfloat16),
        ],
    )(*turned, tail, sums)
    high, deep = lax.axis_size("y_hi"), lax.axis_size("z")
    pieces = coded(found, IMAGE_ROOT).reshape(high, deep, -1, blocks * half)
    pieces = jnp.swapaxes(pieces, 0, 1).reshape(groups, local // groups, blocks * half)
    landed = exchanged(pieces, ("z", "y_hi", "core"))
    landed = landed.reshape(groups // cores, cores, local // groups, blocks * half)
    landed = lax.optimization_barrier(landed)
    mine = decoded(landed, IMAGE_ROOT).sum(0).reshape(cores, local // groups, blocks, half)
    return jnp.concatenate([mine[k] for k in range(cores)], -1)[None]


def solution(mesh):
    sizes = {"y_hi": 4, "z": 8, "core": 2, "y_lo": 2, "x": 4}
    fine = Mesh(mesh.devices.reshape(tuple(sizes.values())), tuple(sizes))
    placed = (P(TM, CHAN), P(None, CHAN, None))
    return jax.shard_map(
        shards, mesh=fine, in_specs=placed, out_specs=P(CHAN, TM, None, None), check_vma=False
    )
```

```python
import functools

import jax
import jax.numpy as jnp
from jax import lax
from jax.experimental import pallas as pl
from jax.experimental.layout import Layout, with_layout_constraint
from jax.experimental.pallas import tpu as pltpu
from jax.sharding import Mesh
from jax.sharding import PartitionSpec as P


TM = ("y_hi", "z", "core")
CHAN = ("y_lo", "x")
ACROSS = ("x", "y_lo")
EDGE = 8
SKETCH_ROOT = 512.0
IMAGE_ROOT = 128.0
LEAST = 1e-30
ANY = pl.BlockSpec(memory_space=pl.ANY)
VMEM = pl.BlockSpec(memory_space=pltpu.VMEM)


def local_kernel(kernel, out_shapes, scratch, in_vmem=True):
    def call(*args):
        if in_vmem:
            args = [pltpu.with_memory_space_constraint(a, pltpu.VMEM) for a in args]
        return pl.pallas_call(
            kernel,
            out_shape=[pltpu.VMEM(shape, dtype) for shape, dtype in out_shapes],
            in_specs=[VMEM if in_vmem else ANY] * len(args),
            out_specs=[VMEM] * len(out_shapes),
            scratch_shapes=scratch,
        )(*args)

    return call


def by_rows(array):
    return with_layout_constraint(array, Layout(tuple(range(array.ndim))))


def exchanged(pieces, axis):
    return lax.all_to_all(pieces, axis, split_axis=0, concat_axis=0, tiled=True)


def coded(values, root_scale):
    root = values * lax.rsqrt(jnp.maximum(jnp.abs(values), LEAST))
    return (root * root_scale).astype(jnp.float16)


def decoded(codes, root_scale):
    root = codes.astype(jnp.float32) * (1.0 / root_scale)
    return root * jnp.abs(root)


def shifted_sum(held, first, reach, width):
    blocks = held.shape[1] // width
    total = held[EDGE + first : EDGE + first + reach, (blocks - 1) * width :]
    for j in range(blocks - 1):
        start = EDGE + first - (blocks - 1 - j)
        total = total + held[start : start + reach, j * width : (j + 1) * width]
    return total


def clear_edges(held, rows):
    held[:EDGE] = jnp.zeros((EDGE, held.shape[1]), jnp.float32)
    held[EDGE + rows :] = jnp.zeros((held.shape[0] - EDGE - rows, held.shape[1]), jnp.float32)


def sketched_own(samples_hbm, sketch_hbm, own_ref, columns_ref, samples_ref, held, arrivals):
    blocks = sketch_hbm.shape[0]
    rows = samples_ref.shape[0]
    reach, width = own_ref.shape
    start = pl.multiple_of(lax.axis_index("core") * width, width)
    step = rows // 2
    rows_loads = [
        pltpu.make_async_copy(
            samples_hbm.at[n : n + step], samples_ref.at[n : n + step], arrivals.at[blocks + n // step]
        )
        for n in range(0, rows, step)
    ]
    loads = [
        pltpu.make_async_copy(
            sketch_hbm.at[j, :, pl.ds(start, width)],
            columns_ref.at[:, j * width : (j + 1) * width],
            arrivals.at[j],
        )
        for j in range(blocks)
    ]
    rows_loads[0].start()
    for load in loads + rows_loads[1:]:
        load.start()
    clear_edges(held, rows)
    for load in loads:
        load.wait()
    for n, load in zip(range(0, rows, step), rows_loads):
        load.wait()
        held[EDGE + n : EDGE + n + step] = jnp.dot(
            samples_ref[n : n + step], columns_ref[...], preferred_element_type=jnp.float32
        )
        end = n + step if n + step < rows else reach
        own_ref[n:end] = shifted_sum(held, n, end - n, width)


def sketched_chip(other_ref, columns_ref, own_ref, out_ref, held):
    rows = other_ref.shape[0]
    reach, width = own_ref.shape
    cores = (out_ref.shape[0] - EDGE) // rows
    clear_edges(held, rows)
    held[EDGE : EDGE + rows] = jnp.dot(
        other_ref[...], columns_ref[...], preferred_element_type=jnp.float32
    )
    core = lax.axis_index("core")
    mine = pl.ds(pl.multiple_of(core * rows, rows), reach)
    theirs = pl.ds(pl.multiple_of((cores - 1 - core) * rows, rows), reach)
    out_ref[...] = jnp.zeros_like(out_ref)
    out_ref[mine] = own_ref[...]
    out_ref[theirs] = out_ref[theirs] + shifted_sum(held, 0, reach, width)


def correlated(block_rows, scale, own_ref, other_ref, tail_ref, sums_ref, out_ref, held, steps):
    reach, width = sums_ref.shape
    rows = own_ref.shape[1]
    cores = reach // rows
    core = lax.axis_index("core")
    mine = pl.ds(pl.multiple_of(core * rows, rows), rows)
    theirs = pl.ds(pl.multiple_of((cores - 1 - core) * rows, rows), rows)
    ends = pl.ds(cores * rows, tail_ref.shape[0])
    depth = cores * rows + 2 * EDGE
    held[:EDGE] = jnp.zeros((EDGE, width), jnp.float32)
    held[EDGE:] = sums_ref[...]
    for i in range(block_rows):
        moved = held[EDGE - 1 - i : EDGE - 1 - i + depth]
        steps[:depth, i * width : (i + 1) * width] = moved.astype(steps.dtype)
    wide = 2 * width
    for i in range(0, block_rows * width, wide):
        found = lax.dot_general(
            tail_ref[...],
            steps[ends, i : i + wide],
            (((0,), (0,)), ((), ())),
            preferred_element_type=jnp.float32,
        )
        for turned, where in ((own_ref, mine), (other_ref, theirs)):
            found = found + jnp.dot(
                turned[...], steps[where, i : i + wide], preferred_element_type=jnp.float32
            )
        out_ref[:, i : i + wide] = found * scale


def shards(samples, sketch):
    rows, local = samples.shape
    blocks, _, width = sketch.shape
    cores = lax.axis_size("core")
    near = lax.axis_size(CHAN)
    groups = lax.axis_size(TM)
    half = width // cores
    part = -(-(cores * rows + blocks - 1) // (near * EDGE)) * EDGE
    reach = near * part
    swap = [(i, cores - 1 - i) for i in range(cores)]
    ahead_route = [(i + cores, i) for i in range(groups - cores)]

    other = by_rows(lax.ppermute(samples, "core", swap))
    held = pltpu.VMEM((rows + 3 * EDGE, blocks * half), jnp.float32)
    own, columns = local_kernel(
        sketched_own,
        [((rows + EDGE, half), jnp.float32), ((local, blocks * half), sketch.dtype)],
        [pltpu.VMEM(samples.shape, samples.dtype), held, pltpu.SemaphoreType.DMA((blocks + 2,))],
        in_vmem=False,
    )(samples, sketch)
    (partial,) = local_kernel(
        sketched_chip, [((reach, half), jnp.float32)], [held]
    )(other, columns, own)
    first = lax.axis_index("core") == 0
    edge = jnp.where(first, samples[:EDGE], other[:EDGE])
    ahead = by_rows(lax.ppermute(edge, TM, ahead_route))
    arrived = exchanged(coded(partial, SKETCH_ROOT).reshape(near, part, half), ACROSS)
    total = decoded(arrived, SKETCH_ROOT).sum(0).astype(jnp.bfloat16)
    total, *turned = lax.optimization_barrier((total, samples.T, other.T))
    tail = jnp.pad(ahead, ((0, EDGE), (0, 0)))
    sums = exchanged(jnp.broadcast_to(total[None], (near, part, half)), ACROSS)
    sums = sums.astype(jnp.float32).reshape(reach, half)
    scale = 1.0 / (rows * groups) ** 0.5
    (found,) = local_kernel(
        functools.partial(correlated, blocks, scale),
        [((local, blocks * half), jnp.float32)],
        [
            pltpu.VMEM((EDGE + reach, half), jnp.float32),
            pltpu.VMEM((cores * rows + 2 * EDGE, blocks * half), jnp.bfloat16),
        ],
    )(*turned, tail, sums)
    pieces = coded(found, IMAGE_ROOT).reshape(groups, local // groups, blocks * half)
    landed = exchanged(pieces, TM)
    landed = landed.reshape(groups // cores, cores, local // groups, blocks * half)
    landed = lax.optimization_barrier(landed)
    mine = decoded(landed, IMAGE_ROOT).sum(0).reshape(cores, local // groups, blocks, half)
    return jnp.concatenate([mine[k] for k in range(cores)], -1)[None]


def solution(mesh):
    sizes = {"y_hi": 4, "z": 8, "core": 2, "y_lo": 2, "x": 4}
    fine = Mesh(mesh.devices.reshape(tuple(sizes.values())), tuple(sizes))
    placed = (P(TM, CHAN), P(None, CHAN, None))
    return jax.shard_map(
        shards, mesh=fine, in_specs=placed, out_specs=P(CHAN, TM, None, None), check_vma=False
    )
```

```python
import functools

import jax
import jax.numpy as jnp
from jax import lax
from jax.experimental import pallas as pl
from jax.experimental.layout import Layout, with_layout_constraint
from jax.experimental.pallas import tpu as pltpu
from jax.sharding import Mesh
from jax.sharding import PartitionSpec as P


TM = ("y_hi", "z", "core")
CHAN = ("y_lo", "x")
EDGE = 8
SKETCH_ROOT = 512.0
IMAGE_ROOT = 128.0
LEAST = 1e-30
ANY = pl.BlockSpec(memory_space=pl.ANY)
VMEM = pl.BlockSpec(memory_space=pltpu.VMEM)


def local_kernel(kernel, out_shapes, scratch, in_vmem=True):
    def call(*args):
        if in_vmem:
            args = [pltpu.with_memory_space_constraint(a, pltpu.VMEM) for a in args]
        return pl.pallas_call(
            kernel,
            out_shape=[pltpu.VMEM(shape, dtype) for shape, dtype in out_shapes],
            in_specs=[VMEM if in_vmem else ANY] * len(args),
            out_specs=[VMEM] * len(out_shapes),
            scratch_shapes=scratch,
        )(*args)

    return call


def by_rows(array):
    return with_layout_constraint(array, Layout(tuple(range(array.ndim))))


def exchanged(pieces, axis):
    return lax.all_to_all(pieces, axis, split_axis=0, concat_axis=0, tiled=True)


def coded(values, root_scale):
    root = values * lax.rsqrt(jnp.maximum(jnp.abs(values), LEAST))
    return (root * root_scale).astype(jnp.float16)


def decoded(codes, root_scale):
    root = codes.astype(jnp.float32) * (1.0 / root_scale)
    return root * jnp.abs(root)


def shifted_sum(held, first, reach, width):
    blocks = held.shape[1] // width
    total = held[EDGE + first : EDGE + first + reach, (blocks - 1) * width :]
    for j in range(blocks - 1):
        start = EDGE + first - (blocks - 1 - j)
        total = total + held[start : start + reach, j * width : (j + 1) * width]
    return total


def clear_edges(held, rows):
    held[:EDGE] = jnp.zeros((EDGE, held.shape[1]), jnp.float32)
    held[EDGE + rows :] = jnp.zeros((held.shape[0] - EDGE - rows, held.shape[1]), jnp.float32)


def sketched_own(samples_hbm, sketch_hbm, own_ref, columns_ref, samples_ref, held, arrivals):
    blocks = sketch_hbm.shape[0]
    rows = samples_ref.shape[0]
    reach, width = own_ref.shape
    start = pl.multiple_of(lax.axis_index("core") * width, width)
    step = rows // 2
    rows_loads = [
        pltpu.make_async_copy(
            samples_hbm.at[n : n + step], samples_ref.at[n : n + step], arrivals.at[blocks + n // step]
        )
        for n in range(0, rows, step)
    ]
    loads = [
        pltpu.make_async_copy(
            sketch_hbm.at[j, :, pl.ds(start, width)],
            columns_ref.at[:, j * width : (j + 1) * width],
            arrivals.at[j],
        )
        for j in range(blocks)
    ]
    rows_loads[0].start()
    for load in loads + rows_loads[1:]:
        load.start()
    clear_edges(held, rows)
    for load in loads:
        load.wait()
    for n, load in zip(range(0, rows, step), rows_loads):
        load.wait()
        held[EDGE + n : EDGE + n + step] = jnp.dot(
            samples_ref[n : n + step], columns_ref[...], preferred_element_type=jnp.float32
        )
        end = n + step if n + step < rows else reach
        own_ref[n:end] = shifted_sum(held, n, end - n, width)


def sketched_chip(other_ref, columns_ref, own_ref, out_ref, held):
    rows = other_ref.shape[0]
    reach, width = own_ref.shape
    cores = (out_ref.shape[0] - EDGE) // rows
    clear_edges(held, rows)
    held[EDGE : EDGE + rows] = jnp.dot(
        other_ref[...], columns_ref[...], preferred_element_type=jnp.float32
    )
    core = lax.axis_index("core")
    mine = pl.ds(pl.multiple_of(core * rows, rows), reach)
    theirs = pl.ds(pl.multiple_of((cores - 1 - core) * rows, rows), reach)
    out_ref[...] = jnp.zeros_like(out_ref)
    out_ref[mine] = own_ref[...]
    out_ref[theirs] = out_ref[theirs] + shifted_sum(held, 0, reach, width)


def correlated(block_rows, scale, own_ref, other_ref, tail_ref, sums_ref, out_ref, held, steps):
    reach, width = sums_ref.shape
    rows = own_ref.shape[1]
    cores = reach // rows
    core = lax.axis_index("core")
    mine = pl.ds(pl.multiple_of(core * rows, rows), rows)
    theirs = pl.ds(pl.multiple_of((cores - 1 - core) * rows, rows), rows)
    ends = pl.ds(cores * rows, tail_ref.shape[0])
    depth = cores * rows + 2 * EDGE
    held[:EDGE] = jnp.zeros((EDGE, width), jnp.float32)
    held[EDGE:] = sums_ref[...]
    for i in range(block_rows):
        moved = held[EDGE - 1 - i : EDGE - 1 - i + depth]
        steps[:depth, i * width : (i + 1) * width] = moved.astype(steps.dtype)
    wide = block_rows * width
    for i in range(0, block_rows * width, wide):
        found = lax.dot_general(
            tail_ref[...],
            steps[ends, i : i + wide],
            (((0,), (0,)), ((), ())),
            preferred_element_type=jnp.float32,
        )
        for turned, where in ((own_ref, mine), (other_ref, theirs)):
            found = found + jnp.dot(
                turned[...], steps[where, i : i + wide], preferred_element_type=jnp.float32
            )
        out_ref[:, i : i + wide] = found * scale


def shards(samples, sketch):
    rows, local = samples.shape
    blocks, _, width = sketch.shape
    cores = lax.axis_size("core")
    near = lax.axis_size(CHAN)
    groups = lax.axis_size(TM)
    half = width // cores
    part = -(-(cores * rows + blocks - 1) // (near * EDGE)) * EDGE
    reach = near * part
    swap = [(i, cores - 1 - i) for i in range(cores)]
    ahead_route = [(i + cores, i) for i in range(groups - cores)]

    other = by_rows(lax.ppermute(samples, "core", swap))
    held = pltpu.VMEM((rows + 3 * EDGE, blocks * half), jnp.float32)
    own, columns = local_kernel(
        sketched_own,
        [((rows + EDGE, half), jnp.float32), ((local, blocks * half), sketch.dtype)],
        [pltpu.VMEM(samples.shape, samples.dtype), held, pltpu.SemaphoreType.DMA((blocks + 2,))],
        in_vmem=False,
    )(samples, sketch)
    (partial,) = local_kernel(
        sketched_chip, [((reach, half), jnp.float32)], [held]
    )(other, columns, own)
    first = lax.axis_index("core") == 0
    edge = jnp.where(first, samples[:EDGE], other[:EDGE])
    ahead = by_rows(lax.ppermute(edge, TM, ahead_route))
    arrived = exchanged(coded(partial, SKETCH_ROOT).reshape(near, part, half), CHAN)
    total = decoded(arrived, SKETCH_ROOT).sum(0).astype(jnp.bfloat16)
    total, *turned = lax.optimization_barrier((total, samples.T, other.T))
    tail = jnp.pad(ahead, ((0, EDGE), (0, 0)))
    sums = exchanged(jnp.broadcast_to(total[None], (near, part, half)), CHAN)
    sums = sums.astype(jnp.float32).reshape(reach, half)
    scale = 1.0 / (rows * groups) ** 0.5
    (found,) = local_kernel(
        functools.partial(correlated, blocks, scale),
        [((local, blocks * half), jnp.float32)],
        [
            pltpu.VMEM((EDGE + reach, half), jnp.float32),
            pltpu.VMEM((cores * rows + 2 * EDGE, blocks * half), jnp.bfloat16),
        ],
    )(*turned, tail, sums)
    pieces = coded(found, IMAGE_ROOT).reshape(groups, local // groups, blocks * half)
    landed = exchanged(pieces, TM)
    landed = landed.reshape(groups // cores, cores, local // groups, blocks * half)
    landed = lax.optimization_barrier(landed)
    mine = decoded(landed, IMAGE_ROOT).sum(0).reshape(cores, local // groups, blocks, half)
    return jnp.concatenate([mine[k] for k in range(cores)], -1)[None]


def solution(mesh):
    sizes = {"y_hi": 4, "z": 8, "core": 2, "y_lo": 2, "x": 4}
    fine = Mesh(mesh.devices.reshape(tuple(sizes.values())), tuple(sizes))
    placed = (P(TM, CHAN), P(None, CHAN, None))
    return jax.shard_map(
        shards, mesh=fine, in_specs=placed, out_specs=P(CHAN, TM, None, None), check_vma=False
    )
```
